128 devices in a mesh: pos: 32 (over x, z, core), tile: 4 (over y).
Axes of the slice: x: 4, y: 4, z: 4, core: 2. Of those that a mesh axis runs over, the one named last changes fastest.
Arguments:
- object_field: float32 [2, 2048, 16384], P(None, 'tile', 'pos'), may hold values from -6 to 6
- probe: float32 [2, 256, 256], replicated, may hold values from -45 to 45
- amplitudes: bfloat16 [4, 32, 32, 256, 256], P('tile', 'pos'), may hold values from 0.099609375 to 3
- corner_rows: int32 [4, 32, 32], P('tile', 'pos'), may hold values from 0 to 511, as said below
- corner_cols: int32 [4, 32, 32], P('tile', 'pos'), may hold values from 0 to 511, as said below
- counts: int32 [4, 32], P('tile', 'pos'), may hold values from 1 to 32, as said below
Outputs:
- object_new: float32 [2, 2048, 16384], P(None, 'tile', 'pos')
- probe_grad: float32 [2, 256, 256], replicated
The draws below stay inside these ranges and needn't reach their ends.
Inputs may be any that keep to these rules, and one draw needn't show every extreme that they name: Slots from counts[t, p] on are unused. `corner_rows`: counted from the first row of the owner's block. `corner_cols`: counted from the first column of the owner's block.
All inputs are finite; a program needn't handle non-finite values.
Results may differ from the reference program's by a relative error of at most 0.0012.
Values sent between devices are 32-bit elements; how exact they have to be, the bound alone decides.
A program may use at most 64 MiB of HBM per device.

```python
import math
import jax
import jax.numpy as jnp
from jax import lax

PATCH = 256
BLOCK_R = 512
BLOCK_C = 512
SLOTS = 32
TILES_T = 4
TILES_P = 32
ROWS_OBJ = 2048
COLS_OBJ = 16384


def draw_counts(key, part):
    first_key, second_key = jax.random.split(key)
    halvings = jax.random.randint(first_key, (TILES_T, TILES_P), 0, 4)
    levels = jnp.maximum(SLOTS // jnp.left_shift(jnp.ones((), jnp.int32), halvings), 1)
    chosen = jax.random.randint(second_key, (), 0, TILES_T * TILES_P)
    flat_levels = levels.reshape(TILES_T * TILES_P).at[chosen].set(SLOTS)
    return flat_levels.reshape(TILES_T, TILES_P).astype(jnp.int32)


def corner_draw(key, upper_end):
    first_key, second_key = jax.random.split(key)
    slot_total = TILES_T * TILES_P * SLOTS
    corners = jax.random.randint(first_key, (slot_total,), 0, upper_end)
    chosen = jax.random.randint(second_key, (), 0, slot_total)
    corners = corners.at[chosen].set(upper_end - 1).at[(chosen + 1) % slot_total].set(0)
    return corners.reshape(TILES_T, TILES_P, SLOTS).astype(jnp.int32)


def draw_corner_rows(key, part):
    return corner_draw(jax.random.fold_in(key, 11), BLOCK_R)


def draw_corner_cols(key, part):
    return corner_draw(jax.random.fold_in(key, 23), BLOCK_C)


def draw_probe(key, part):
    key_list = jax.random.split(jax.random.fold_in(key, 37), 3)
    log_low = math.log(0.3)
    log_high = math.log(3.0)
    row_scale = jnp.exp(jax.random.uniform(key_list[1], (1, PATCH, 1), jnp.float32, log_low, log_high))
    col_scale = jnp.exp(jax.random.uniform(key_list[2], (1, 1, PATCH), jnp.float32, log_low, log_high))
    entries = jnp.clip(jax.random.normal(key_list[0], (2, PATCH, PATCH), jnp.float32), -5.0, 5.0)
    return (entries * row_scale * col_scale).astype(jnp.float32)


def shard_levels(own_key, shape, cuts, least, top_value):
    loudness, own = 1.0, jax.random.fold_in(own_key, 6)
    for axis_at, blocks in cuts:
        heights = jnp.exp(jax.random.uniform(jax.random.fold_in(own, axis_at), (blocks,), jnp.float32, least / len(cuts), top_value / len(cuts)))
        loudness = loudness * jnp.repeat(heights, shape[axis_at] // blocks).reshape([-1 if axis == axis_at else 1 for axis in range(len(shape))])
    return loudness


def gaussian(stream_key, extent, scale, most, pieces=(), kind=jnp.bfloat16):
    values = jax.random.normal(stream_key, extent, jnp.float32) * scale
    if len(pieces) > 0:
        values = shard_levels(stream_key, extent, pieces, -0.22, 0.18) * values
    return jnp.clip(values, min=-most, max=most).astype(kind)


def setup_inputs(seed: int = 0) -> dict:
    splits = jax.random.split(jax.random.key(seed), 7)
    object_field = gaussian(splits[0], (2, ROWS_OBJ, COLS_OBJ), 1.0, 6.0, ((1, 4), (2, 32)), jnp.float32)
    probe = draw_probe(jax.random.fold_in(splits[6], 71), 0)
    amplitudes = jnp.clip(jnp.exp(math.log(3.0) - 3.4051113 * jax.random.uniform(splits[2], (TILES_T, TILES_P, SLOTS, PATCH, PATCH), jnp.float32) ** shard_levels(splits[2], (TILES_T, TILES_P, SLOTS, PATCH, PATCH), ((0, 4), (1, 32)), -0.2, 0.2)), 0.099609375, 3.0).astype(jnp.bfloat16)
    corner_rows = draw_corner_rows(jax.random.fold_in(splits[6], 71), 0)
    corner_cols = draw_corner_cols(jax.random.fold_in(splits[6], 71), 0)
    counts = draw_counts(jax.random.fold_in(splits[6], 71), 0)
    return {"object_field": object_field, "probe": probe, "amplitudes": amplitudes, "corner_rows": corner_rows, "corner_cols": corner_cols, "counts": counts}


def dft_tables(points):
    indices = jnp.arange(points, dtype=jnp.int32)
    residues = indices[:, None] * indices[None, :] % points
    angles = residues.astype(jnp.float32) * (2.0 * math.pi / points)
    factor = 1.0 / math.sqrt(points)
    return ((jnp.cos(angles) * factor).astype(jnp.bfloat16), (-jnp.sin(angles) * factor).astype(jnp.bfloat16))

def left_product(table_re, table_im, part_re, part_im):

    def product(matrix, operand):
        return jnp.dot(matrix, operand, preferred_element_type=jnp.float32)
    return (product(table_re, part_re) - product(table_im, part_im), product(table_re, part_im) + product(table_im, part_re))

def right_product(part_re, part_im, table_re, table_im):

    def product(operand, matrix):
        return jnp.dot(operand, matrix, preferred_element_type=jnp.float32)
    return (product(part_re, table_re) - product(part_im, table_im), product(part_re, table_im) + product(part_im, table_re))

def propagate(exit_re, exit_im, amplitude, table_re, table_im):
    near_re, near_im = left_product(table_re, table_im, exit_re.astype(jnp.bfloat16), exit_im.astype(jnp.bfloat16))
    far_re, far_im = right_product(near_re.astype(jnp.bfloat16), near_im.astype(jnp.bfloat16), table_re, table_im)
    modulus = jnp.sqrt(far_re * far_re + far_im * far_im + 0.25)
    ratio = amplitude.astype(jnp.float32) / modulus
    back_re, back_im = left_product(table_re, -table_im, (far_re * ratio).astype(jnp.bfloat16), (far_im * ratio).astype(jnp.bfloat16))
    new_re, new_im = right_product(back_re.astype(jnp.bfloat16), back_im.astype(jnp.bfloat16), table_re, -table_im)
    return (new_re - exit_re, new_im - exit_im)

def reference(object_field, probe, amplitudes, corner_rows, corner_cols, counts):
    table_re, table_im = dft_tables(PATCH)
    padded = jnp.pad(object_field, ((0, 0), (0, PATCH), (0, PATCH)))
    per_owner = TILES_P * SLOTS
    total_slots = TILES_T * per_owner
    probe_re, probe_im = (probe[0], probe[1])

    def slot_terms(operands):
        patch_re, patch_im, amplitude = operands
        exit_re = probe_re * patch_re - probe_im * patch_im
        exit_im = probe_re * patch_im + probe_im * patch_re
        delta_re, delta_im = propagate(exit_re, exit_im, amplitude, table_re, table_im)
        object_part = jnp.stack([probe_re * delta_re + probe_im * delta_im, probe_re * delta_im - probe_im * delta_re])
        probe_part = jnp.stack([patch_re * delta_re + patch_im * delta_im, patch_re * delta_im - patch_im * delta_re])
        return (object_part, probe_part)

    def skip_terms(operands):
        zeros_pair = jnp.zeros((2, PATCH, PATCH), jnp.float32)
        return (zeros_pair, zeros_pair)

    def visit(slot_index, state_pair):
        update, probe_sum = state_pair
        slot_index = slot_index.astype(jnp.int32)
        owner_t = slot_index // per_owner
        owner_p = slot_index // SLOTS % TILES_P
        slot_pos = slot_index % SLOTS
        row_start = (owner_t * BLOCK_R + corner_rows[owner_t, owner_p, slot_pos]).astype(jnp.int32)
        col_start = (owner_p * BLOCK_C + corner_cols[owner_t, owner_p, slot_pos]).astype(jnp.int32)
        zero_index = jnp.zeros((), jnp.int32)
        window = lax.dynamic_slice(padded, (zero_index, row_start, col_start), (2, PATCH, PATCH))
        amplitude = amplitudes[owner_t, owner_p, slot_pos]
        object_part, probe_part = lax.cond(slot_pos < counts[owner_t, owner_p], slot_terms, skip_terms, (window[0], window[1], amplitude))
        current = lax.dynamic_slice(update, (zero_index, row_start, col_start), (2, PATCH, PATCH))
        update = lax.dynamic_update_slice(update, current + object_part, (zero_index, row_start, col_start))
        return (update, probe_sum + probe_part)
    start_state = (jnp.zeros(padded.shape, jnp.float32), jnp.zeros((2, PATCH, PATCH), jnp.float32))
    update, probe_sum = lax.fori_loop(0, total_slots, visit, start_state)
    update = update[:, :ROWS_OBJ, :COLS_OBJ]
    power = jnp.mean(probe_re * probe_re + probe_im * probe_im) + 1e-06
    object_new = object_field + update / power
    probe_grad = probe_sum / math.sqrt(total_slots)
    return (object_new, probe_grad)
```

```python
import functools

import jax
import jax.numpy as jnp
import ml_dtypes
import numpy as np
from jax import lax
from jax.experimental import pallas as pl
from jax.experimental.pallas import tpu as pltpu
from jax.sharding import PartitionSpec as P

N = 256
H = 128
BLOCK = 512
WIDE = 768


def dft_tables():
    j = np.arange(N)
    angle = (j[:, None] * j[None, :] % N) * (2.0 * np.pi / N)
    re = (np.cos(angle) / np.sqrt(N)).astype(np.float32).astype(ml_dtypes.bfloat16)
    im = (-np.sin(angle) / np.sqrt(N)).astype(np.float32).astype(ml_dtypes.bfloat16)
    return re, im


def stage_tables():
    re, im = dft_tables()

    def pair(a, b, c, d):
        return np.concatenate([np.concatenate([a, b], 1), np.concatenate([c, d], 1)], 0)

    first = [pair(re[:H, q::2], -im[:H, q::2], im[:H, q::2], re[:H, q::2]) for q in (0, 1)]
    second = pair(re, im, -im, re)
    third = [pair(re[q::2, :H], im[q::2, :H], -im[q::2, :H], re[q::2, :H]) for q in (0, 1)]
    fourth = pair(re, -im, im, re)
    return np.stack(first), second, np.stack(third), fourth


def slots_kernel(
    rule, row_base, places,
    rows_ref, cols_ref, count_ref,
    probe_ref, amp_ref, t1_ref, t2_ref, t3_ref, t4_ref, *refs,
):
    n_pieces = len(places)
    pieces = refs[:n_pieces]
    upd_ref, psum_ref = refs[n_pieces : n_pieces + 2]
    (ext, prb_raw, prb, pat, ext_b, exit_s, near_b, fold_b, back_b, amp_buf, order, piece_sem, amp_sem) = refs[n_pieces + 2 :]

    copies = []

    def bring(source, target):
        copies.append(pltpu.make_async_copy(source, target, piece_sem.at[len(copies)]))
        copies[-1].start()

    for b in range(2):
        bring(probe_ref.at[:, :, b * H : (b + 1) * H], prb_raw.at[:, b])
    for piece, (r0, c0) in zip(pieces, places):
        _, h, w = piece.shape
        for b in range(w // H):
            bring(piece.at[:, :, b * H : (b + 1) * H], ext.at[:, c0 // H + b, r0 : r0 + h, :])

    def collect(s, n):
        order[n] = s
        keep = jnp.logical_and(s < count_ref[0, 0], rule(rows_ref[0, 0, s], cols_ref[0, 0, s]))
        return n + keep.astype(jnp.int32)

    total = lax.fori_loop(0, rows_ref.shape[2], collect, jnp.int32(0))

    def amp_copy(i):
        slot = lax.rem(i, 2)
        return pltpu.make_async_copy(amp_ref.at[0, 0, order[i]], amp_buf.at[slot], amp_sem.at[slot])

    @pl.when(total > 0)
    def _():
        amp_copy(0).start()

    upd_ref[...] = jnp.zeros_like(upd_ref)
    psum_ref[...] = jnp.zeros_like(psum_ref)
    for copy in copies:
        copy.wait()
    for comp in range(2):
        for q in range(2):
            for b in range(2):
                prb[comp, q * H : (q + 1) * H, b * H : (b + 1) * H] = prb_raw[comp, b, pl.ds(q, H, stride=2), :]

    lane = lax.broadcasted_iota(jnp.int32, (H, H), 1)

    def step(i, carry):
        s = order[i]
        r = rows_ref[0, 0, s] - row_base
        c = cols_ref[0, 0, s]
        off = lax.rem(c, H)
        c0 = c // H
        back_shift = lax.rem(H - off, H)

        @pl.when(i + 1 < total)
        def _():
            amp_copy(i + 1).start()

        for q in range(2):
            part = []
            for comp in range(2):
                blocks = [
                    pltpu.roll(ext[comp, c0 + b, pl.ds(r + q, H, stride=2), :], back_shift, 1)
                    for b in range(3)
                ]
                part.append(
                    [jnp.where(lane < H - off, blocks[b], blocks[b + 1]) for b in range(2)]
                )
            for b in range(2):
                here = (slice(q * H, (q + 1) * H), slice(b * H, (b + 1) * H))
                pre, pim = prb[0][here], prb[1][here]
                are, aim = part[0][b], part[1][b]
                ere = pre * are - pim * aim
                eim = pre * aim + pim * are
                pat[(0,) + here] = are
                pat[(1,) + here] = aim
                exit_s[(0,) + here] = ere
                exit_s[(1,) + here] = eim
                ext_b[q, 0:H, b * H : (b + 1) * H] = ere.astype(jnp.bfloat16)
                ext_b[q, H:N, b * H : (b + 1) * H] = eim.astype(jnp.bfloat16)

        dot = functools.partial(jnp.dot, preferred_element_type=jnp.float32)
        even = dot(t1_ref[0], ext_b[0])
        odd = dot(t1_ref[1], ext_b[1])
        for comp in range(2):
            e, o = even[comp * H : (comp + 1) * H], odd[comp * H : (comp + 1) * H]
            near_b[0:H, comp * N : (comp + 1) * N] = (e + o).astype(jnp.bfloat16)
            near_b[H:N, comp * N : (comp + 1) * N] = (e - o).astype(jnp.bfloat16)

        amp_copy(i).wait()
        amp = amp_buf.at[lax.rem(i, 2)]
        far = dot(near_b[...], t2_ref[...])
        fre, fim = far[:, :N], far[:, N:]
        ratio = amp[...].astype(jnp.float32) * lax.rsqrt(fre * fre + fim * fim + 0.25)
        for comp, part in enumerate((fre * ratio, fim * ratio)):
            top, low = part[:H], part[H:]
            fold_b[0, comp * H : (comp + 1) * H, :] = (top + low).astype(jnp.bfloat16)
            fold_b[1, comp * H : (comp + 1) * H, :] = (top - low).astype(jnp.bfloat16)

        for q in range(2):
            back = dot(t3_ref[q], fold_b[q])
            for comp in range(2):
                back_b[q * H : (q + 1) * H, comp * N : (comp + 1) * N] = back[comp * H : (comp + 1) * H].astype(
                    jnp.bfloat16
                )
        new = dot(back_b[...], t4_ref[...])
        dre = new[:, :N] - exit_s[0]
        dim = new[:, N:] - exit_s[1]
        psum_ref[0] += pat[0] * dre + pat[1] * dim
        psum_ref[1] += pat[0] * dim - pat[1] * dre
        terms = (prb[0] * dre + prb[1] * dim, prb[0] * dim - prb[1] * dre)
        for comp in range(2):
            for q in range(2):
                z0 = pltpu.roll(terms[comp][q * H : (q + 1) * H, :H], off, 1)
                z1 = pltpu.roll(terms[comp][q * H : (q + 1) * H, H:], off, 1)
                zero = jnp.zeros_like(z0)
                for b, val in enumerate(
                    (jnp.where(lane >= off, z0, zero), jnp.where(lane >= off, z1, z0), jnp.where(lane >= off, zero, z1))
                ):
                    here = (comp, c0 + b, pl.ds(r + q, H, stride=2), slice(None))
                    upd_ref[here] = upd_ref[here] + val
        return carry

    lax.fori_loop(0, total, step, 0)


def run_slots(rule, row_base, height, places, pieces, scalars, probe, amplitudes, tables):
    smem = pl.BlockSpec(memory_space=pltpu.SMEM)
    vmem = pl.BlockSpec(memory_space=pltpu.VMEM)
    hbm = pl.BlockSpec(memory_space=pl.ANY)
    return pl.pallas_call(
        functools.partial(slots_kernel, rule, row_base, places),
        out_shape=(
            jax.ShapeDtypeStruct((2, WIDE // H, height, H), jnp.float32),
            jax.ShapeDtypeStruct((2, N, N), jnp.float32),
        ),
        in_specs=[smem] * 3 + [hbm, hbm] + [vmem] * 4 + [hbm] * len(pieces),
        out_specs=(vmem, vmem),
        scratch_shapes=[
            pltpu.VMEM((2, WIDE // H, height, H), jnp.float32),
            pltpu.VMEM((2, 2, N, H), jnp.float32),
            pltpu.VMEM((2, N, N), jnp.float32),
            pltpu.VMEM((2, N, N), jnp.float32),
            pltpu.VMEM((2, N, N), jnp.bfloat16),
            pltpu.VMEM((2, N, N), jnp.float32),
            pltpu.VMEM((N, 2 * N), jnp.bfloat16),
            pltpu.VMEM((2, N, N), jnp.bfloat16),
            pltpu.VMEM((N, 2 * N), jnp.bfloat16),
            pltpu.VMEM((2, N, N), jnp.bfloat16),
            pltpu.SMEM((40,), jnp.int32),
            pltpu.SemaphoreType.DMA((2 + sum(p.shape[2] // H for p in pieces),)),
            pltpu.SemaphoreType.DMA((2,)),
        ],
        compiler_params=pltpu.CompilerParams(vmem_limit_bytes=40 * 1024 * 1024),
        cost_estimate=pl.CostEstimate(flops=12_000_000_000, bytes_accessed=16_000_000, transcendentals=0),
    )(*scalars, probe, amplitudes, *tables, *pieces)


def passed_along(block, axis, distance):
    devices = range(lax.axis_size(axis))
    route = [(i - distance, i) for i in devices if i - distance in devices]
    return lax.ppermute(block, axis, route)


def interleave(pair):
    return pair.reshape(2, 2, H, N).transpose(0, 2, 1, 3).reshape(2, N, N)


def shards(object_field, probe, amplitudes, corner_rows, corner_cols, counts):
    tables = [jnp.asarray(t) for t in stage_tables()]
    slot_total = corner_rows.shape[2]
    lower = passed_along(object_field[:, :N, :], "tile", -1)
    right = passed_along(object_field[:, :, :N], "pos", -1)
    corner = passed_along(lower[:, :, :N], "pos", -1)
    scalars = (corner_rows, corner_cols, counts)
    upd1, sum1 = run_slots(
        lambda r, c: r <= BLOCK - N, 0, BLOCK, ((0, 0), (0, BLOCK)), (object_field, right),
        scalars, probe, amplitudes, tables,
    )
    upd2, sum2 = run_slots(
        lambda r, c: r > BLOCK - N, N, BLOCK, ((0, 0), (0, BLOCK), (N, 0), (N, BLOCK)),
        (object_field[:, N:, :], right[:, N:, :], lower, corner),
        scalars, probe, amplitudes, tables,
    )
    upd1, upd2 = (u.transpose(0, 2, 1, 3).reshape(2, BLOCK, WIDE) for u in (upd1, upd2))
    update = jnp.pad(upd1, ((0, 0), (0, N), (0, 0))) + jnp.pad(upd2, ((0, 0), (N, 0), (0, 0)))
    right_back = passed_along(update[:, :, BLOCK:], "pos", 1)
    main_part = update[:, :, :BLOCK].at[:, :, :N].add(right_back)
    lower_back = passed_along(main_part[:, BLOCK:, :], "tile", 1)
    owned_update = main_part[:, :BLOCK, :].at[:, :N, :].add(lower_back)
    probe_total = lax.psum(interleave(sum1 + sum2), ("pos", "tile"))
    power = jnp.mean(probe[0] * probe[0] + probe[1] * probe[1]) + 1e-06
    object_new = object_field + owned_update / power
    probe_grad = probe_total / np.sqrt(lax.axis_size("pos") * lax.axis_size("tile") * slot_total).astype(np.float32)
    return (object_new, probe_grad)


def solution(mesh):
    return jax.shard_map(
        shards,
        mesh=mesh,
        in_specs=(
            P(None, "tile", "pos"),
            P(),
            P("tile", "pos", None, None, None),
            P("tile", "pos", None),
            P("tile", "pos", None),
            P("tile", "pos"),
        ),
        out_specs=(P(None, "tile", "pos"), P()),
        check_vma=False,
    )
```

```python
import functools
import math

import jax
import jax.numpy as jnp
import ml_dtypes
import numpy as np
from jax import lax
from jax.experimental import pallas as pl
from jax.experimental.pallas import tpu as pltpu
from jax.sharding import PartitionSpec as P

N = 256
H = 128
BLOCK = 512
WIDE = 768


def dft_tables():
    j = np.arange(N)
    angle = (j[:, None] * j[None, :] % N) * (2.0 * np.pi / N)
    re = (np.cos(angle) / np.sqrt(N)).astype(np.float32).astype(ml_dtypes.bfloat16)
    im = (-np.sin(angle) / np.sqrt(N)).astype(np.float32).astype(ml_dtypes.bfloat16)
    return re, im


def stage_tables():
    re, im = dft_tables()

    def pair(a, b, c, d):
        return np.concatenate([np.concatenate([a, b], 1), np.concatenate([c, d], 1)], 0)

    first = [pair(re[:H, q::2], -im[:H, q::2], im[:H, q::2], re[:H, q::2]) for q in (0, 1)]
    second = pair(re, im, -im, re)
    third = [pair(re[q::2, :H], im[q::2, :H], -im[q::2, :H], re[q::2, :H]) for q in (0, 1)]
    fourth = pair(re, -im, im, re)
    return np.stack(first), second, np.stack(third), fourth


def slots_kernel(
    rule, row_base, places, follows,
    rows_ref, cols_ref, count_ref,
    probe_ref, amp_ref, t1_ref, t2_ref, t3_ref, t4_ref, *refs,
):
    n_pieces = len(places)
    pieces = refs[:n_pieces]
    refs = refs[n_pieces:]
    if follows:
        before = refs[:2]
        refs = refs[2:]
    upd_ref, psum_ref = refs[:2]
    (ext, prb_raw, prb, pat, ext_b, exit_s, near_b, fold_b, back_b, amp_buf, order, piece_sem, amp_sem) = refs[2:]

    copies = []

    def bring(source, target):
        copies.append(pltpu.make_async_copy(source, target, piece_sem.at[len(copies)]))
        copies[-1].start()

    for b in range(2):
        bring(probe_ref.at[:, :, b * H : (b + 1) * H], prb_raw.at[:, b])
    for piece, (r0, c0) in zip(pieces, places):
        _, h, w = piece.shape
        for b in range(w // H):
            bring(piece.at[:, :, b * H : (b + 1) * H], ext.at[:, c0 // H + b, r0 : r0 + h, :])

    def collect(s, n):
        order[n] = s
        keep = jnp.logical_and(s < count_ref[0, 0], rule(rows_ref[0, 0, s], cols_ref[0, 0, s]))
        return n + keep.astype(jnp.int32)

    total = lax.fori_loop(0, rows_ref.shape[2], collect, jnp.int32(0))

    def amp_copy(i):
        slot = lax.rem(i, 2)
        return pltpu.make_async_copy(amp_ref.at[0, 0, order[i]], amp_buf.at[slot], amp_sem.at[slot])

    @pl.when(total > 0)
    def _():
        amp_copy(0).start()

    if follows:
        bring(before[0].at[:, :, N:, :], upd_ref.at[:, :, :N, :])
        bring(before[1], psum_ref)
        upd_ref[:, :, N:, :] = jnp.zeros((2, WIDE // H, N, H), jnp.float32)
    else:
        upd_ref[...] = jnp.zeros_like(upd_ref)
        psum_ref[...] = jnp.zeros_like(psum_ref)
    for copy in copies:
        copy.wait()
    for comp in range(2):
        for q in range(2):
            for b in range(2):
                prb[comp, q * H : (q + 1) * H, b * H : (b + 1) * H] = prb_raw[comp, b, pl.ds(q, H, stride=2), :]

    lane = lax.broadcasted_iota(jnp.int32, (H, H), 1)

    def step(i, carry):
        s = order[i]
        r = rows_ref[0, 0, s] - row_base
        c = cols_ref[0, 0, s]
        off = lax.rem(c, H)
        c0 = c // H
        back_shift = lax.rem(H - off, H)

        @pl.when(i + 1 < total)
        def _():
            amp_copy(i + 1).start()

        for q in range(2):
            part = []
            for comp in range(2):
                blocks = [
                    pltpu.roll(ext[comp, c0 + b, pl.ds(r + q, H, stride=2), :], back_shift, 1)
                    for b in range(3)
                ]
                part.append(
                    [jnp.where(lane < H - off, blocks[b], blocks[b + 1]) for b in range(2)]
                )
            for b in range(2):
                here = (slice(q * H, (q + 1) * H), slice(b * H, (b + 1) * H))
                pre, pim = prb[0][here], prb[1][here]
                are, aim = part[0][b], part[1][b]
                ere = pre * are - pim * aim
                eim = pre * aim + pim * are
                pat[(0,) + here] = are
                pat[(1,) + here] = aim
                exit_s[(0,) + here] = ere
                exit_s[(1,) + here] = eim
                ext_b[q, 0:H, b * H : (b + 1) * H] = ere.astype(jnp.bfloat16)
                ext_b[q, H:N, b * H : (b + 1) * H] = eim.astype(jnp.bfloat16)

        dot = functools.partial(jnp.dot, preferred_element_type=jnp.float32)
        even = dot(t1_ref[0], ext_b[0])
        odd = dot(t1_ref[1], ext_b[1])
        for comp in range(2):
            e, o = even[comp * H : (comp + 1) * H], odd[comp * H : (comp + 1) * H]
            near_b[0:H, comp * N : (comp + 1) * N] = (e + o).astype(jnp.bfloat16)
            near_b[H:N, comp * N : (comp + 1) * N] = (e - o).astype(jnp.bfloat16)

        amp_copy(i).wait()
        amp = amp_buf.at[lax.rem(i, 2)]
        far = dot(near_b[...], t2_ref[...])
        fre, fim = far[:, :N], far[:, N:]
        ratio = amp[...].astype(jnp.float32) * lax.rsqrt(fre * fre + fim * fim + 0.25)
        for comp, part in enumerate((fre * ratio, fim * ratio)):
            top, low = part[:H], part[H:]
            fold_b[0, comp * H : (comp + 1) * H, :] = (top + low).astype(jnp.bfloat16)
            fold_b[1, comp * H : (comp + 1) * H, :] = (top - low).astype(jnp.bfloat16)

        for q in range(2):
            back = dot(t3_ref[q], fold_b[q])
            for comp in range(2):
                back_b[q * H : (q + 1) * H, comp * N : (comp + 1) * N] = back[comp * H : (comp + 1) * H].astype(
                    jnp.bfloat16
                )
        new = dot(back_b[...], t4_ref[...])
        dre = new[:, :N] - exit_s[0]
        dim = new[:, N:] - exit_s[1]
        psum_ref[0] += pat[0] * dre + pat[1] * dim
        psum_ref[1] += pat[0] * dim - pat[1] * dre
        terms = (prb[0] * dre + prb[1] * dim, prb[0] * dim - prb[1] * dre)
        for comp in range(2):
            for q in range(2):
                z0 = pltpu.roll(terms[comp][q * H : (q + 1) * H, :H], off, 1)
                z1 = pltpu.roll(terms[comp][q * H : (q + 1) * H, H:], off, 1)
                zero = jnp.zeros_like(z0)
                for b, val in enumerate(
                    (jnp.where(lane >= off, z0, zero), jnp.where(lane >= off, z1, z0), jnp.where(lane >= off, zero, z1))
                ):
                    here = (comp, c0 + b, pl.ds(r + q, H, stride=2), slice(None))
                    upd_ref[here] = upd_ref[here] + val
        return carry

    lax.fori_loop(0, total, step, 0)
    if follows:
        for comp in range(2):
            for b in range(2):
                lanes = slice(b * H, (b + 1) * H)
                for q in range(2):
                    prb_raw[comp, b, pl.ds(q, H, stride=2), :] = psum_ref[comp, q * H : (q + 1) * H, lanes]
                psum_ref[comp, :, lanes] = prb_raw[comp, b]


def run_slots(rule, row_base, height, places, pieces, before, scalars, probe, amplitudes, tables):
    smem = pl.BlockSpec(memory_space=pltpu.SMEM)
    vmem = pl.BlockSpec(memory_space=pltpu.VMEM)
    hbm = pl.BlockSpec(memory_space=pl.ANY)
    return pl.pallas_call(
        functools.partial(slots_kernel, rule, row_base, places, bool(before)),
        out_shape=(
            jax.ShapeDtypeStruct((2, WIDE // H, height, H), jnp.float32),
            jax.ShapeDtypeStruct((2, N, N), jnp.float32),
        ),
        in_specs=[smem] * 3 + [hbm, hbm] + [vmem] * 4 + [hbm] * (len(pieces) + len(before)),
        out_specs=(vmem, vmem),
        scratch_shapes=[
            pltpu.VMEM((2, WIDE // H, height, H), jnp.float32),
            pltpu.VMEM((2, 2, N, H), jnp.float32),
            pltpu.VMEM((2, N, N), jnp.float32),
            pltpu.VMEM((2, N, N), jnp.float32),
            pltpu.VMEM((2, N, N), jnp.bfloat16),
            pltpu.VMEM((2, N, N), jnp.float32),
            pltpu.VMEM((N, 2 * N), jnp.bfloat16),
            pltpu.VMEM((2, N, N), jnp.bfloat16),
            pltpu.VMEM((N, 2 * N), jnp.bfloat16),
            pltpu.VMEM((2, N, N), jnp.bfloat16),
            pltpu.SMEM((40,), jnp.int32),
            pltpu.SemaphoreType.DMA((4 + sum(p.shape[2] // H for p in pieces),)),
            pltpu.SemaphoreType.DMA((2,)),
        ],
        compiler_params=pltpu.CompilerParams(vmem_limit_bytes=40 * 1024 * 1024),
        cost_estimate=pl.CostEstimate(flops=12_000_000_000, bytes_accessed=16_000_000, transcendentals=0),
    )(*scalars, probe, amplitudes, *tables, *pieces, *before)


def passed_along(block, axis, distance):
    devices = range(lax.axis_size(axis))
    route = [(i - distance, i) for i in devices if i - distance in devices]
    return lax.ppermute(block, axis, route)


def exchange_kernel(
    first_ref, second_ref, obj_ref, sum_ref, probe_ref, out_ref, grad_ref,
    from_left, from_above, corner, pair_in, part, x_in, piece, tile_in, gathered,
    right_send, right_recv, low_send, low_recv, pair_send, pair_recv, x_send, x_recv,
    t_send, t_recv, tg_send, tg_recv, xg_send, xg_recv, cg_send, cg_recv,
):
    p = lax.axis_index("pos")
    t = lax.axis_index("tile")
    x, z, core = p // 8, (p // 2) % 4, p % 2
    g = z * 4 + t

    def pos_of(xx, zz, cc):
        return xx * 8 + zz * 2 + cc

    right = {"pos": (p + 1) % 32, "tile": t}
    left = {"pos": (p + 31) % 32, "tile": t}
    below = {"pos": p, "tile": (t + 1) % 4}
    partner = {"pos": pos_of(x, z, 1 - core), "tile": t}
    x_peers = [{"pos": pos_of((x + d) % 4, z, core), "tile": t} for d in (1, 2, 3)]
    g_peers = [{"pos": pos_of(x, ((g + d) % 16) // 4, core), "tile": (g + d) % 4} for d in range(1, 16)]

    barrier = pltpu.get_barrier_semaphore()
    for peer in [right, left, partner] + x_peers + g_peers:
        pl.semaphore_signal(barrier, inc=1, device_id=peer, device_id_type=pl.DeviceIdType.MESH)
    pl.semaphore_wait(barrier, 21)

    started = []

    def send(source, target, send_sem, recv_sem, peer):
        copy = pltpu.make_async_remote_copy(
            src_ref=source, dst_ref=target, send_sem=send_sem, recv_sem=recv_sem,
            device_id=peer, device_id_type=pl.DeviceIdType.MESH,
        )
        copy.start()
        started.append(copy)
        return copy

    edge = send(second_ref.at[:, 4:6, N:, :], from_left.at[:, :, 2 * N :, :], right_send.at[0], right_recv.at[0], right)
    low1 = send(second_ref.at[:, 2:4, N:, :], from_above.at[:, 2:4], low_send.at[0], low_recv.at[0], below)
    half = send(sum_ref.at[pl.ds((1 - core) * N, N)], pair_in, pair_send.at[0], pair_recv.at[0], partner)
    mid = send(second_ref.at[:, 4:6, :N, :], from_left.at[:, :, N : 2 * N, :], right_send.at[1], right_recv.at[1], right)
    top = send(first_ref.at[:, 4:6, :N, :], from_left.at[:, :, :N, :], right_send.at[2], right_recv.at[2], right)

    half.wait_recv()
    part[...] = sum_ref[pl.ds(core * N, N), :] + pair_in[...]
    x_copies = [
        send(part.at[pl.ds(((x + d) % 4) * 64, 64)], x_in.at[d - 1], x_send.at[d - 1], x_recv.at[d - 1], x_peers[d - 1])
        for d in (1, 2, 3)
    ]

    edge.wait_recv()
    has_left = (p > 0).astype(jnp.float32)
    has_above = (t > 0).astype(jnp.float32)
    corner[...] = second_ref[:, 0:2, N:, :] + from_left[:, :, 2 * N :, :] * has_left
    low0 = send(corner, from_above.at[:, 0:2], low_send.at[1], low_recv.at[1], below)

    for copy in x_copies:
        copy.wait_recv()
    shard = part[pl.ds(x * 64, 64), :] + x_in[0] + x_in[1] + x_in[2]
    for rg in range(8):
        for lg in range(2):
            piece[rg * 2 + lg] = shard[rg * 8 : rg * 8 + 8, lg * H : (lg + 1) * H]
    t_copies = [
        send(piece.at[(g + d) % 16], tile_in.at[d - 1], t_send.at[d - 1], t_recv.at[d - 1], g_peers[d - 1])
        for d in range(1, 16)
    ]
    power = jnp.sum(probe_ref[...] * probe_ref[...]) * (1.0 / (N * N)) + 1e-06
    scale = 1.0 / jnp.full((1, H), power, jnp.float32)

    for copy in t_copies:
        copy.wait_recv()
    own = piece[g]
    for d in range(15):
        own = own + tile_in[d]
    slots = 128 * 32
    gathered[core, x, g] = own * np.float32(1.0 / math.sqrt(slots))
    tg_copies = [
        send(gathered.at[core, x, g], gathered.at[core, x, g], tg_send.at[d - 1], tg_recv.at[d - 1], g_peers[d - 1])
        for d in range(1, 16)
    ]

    for copy in tg_copies:
        copy.wait_recv()
    xg_copies = [
        send(gathered.at[core, x], gathered.at[core, x], xg_send.at[d - 1], xg_recv.at[d - 1], x_peers[d - 1])
        for d in (1, 2, 3)
    ]
    cg_copies = [send(gathered.at[core, x], gathered.at[core, x], cg_send.at[0], cg_recv.at[0], partner)]

    def put(b, r0, value):
        for comp in range(2):
            here = (comp, slice(r0, r0 + N), slice(b * H, (b + 1) * H))
            out_ref[here] = obj_ref[here] + value[comp] * scale

    for b in (2, 3):
        put(b, N, second_ref[:, b, :N, :])
    for d in (1, 2, 3):
        xg_copies[d - 1].wait_recv()
        came = (x + 4 - d) % 4
        cg_copies.append(
            send(gathered.at[core, came], gathered.at[core, came], cg_send.at[d], cg_recv.at[d], partner)
        )
    mid.wait_recv()
    for b in (0, 1):
        put(b, N, second_ref[:, b, :N, :] + from_left[:, b, N : 2 * N, :] * has_left)
    low1.wait_recv()
    for b in (2, 3):
        put(b, 0, first_ref[:, b, :N, :] + from_above[:, b] * has_above)
    top.wait_recv()
    for copy in cg_copies:
        copy.wait_recv()
    for h in range(2):
        for xx in range(4):
            for rg in range(8):
                for lg in range(2):
                    grad_ref[h, xx * 64 + rg * 8 : xx * 64 + rg * 8 + 8, lg * H : (lg + 1) * H] = gathered[h, xx, rg * 2 + lg]
    low0.wait_recv()
    for b in (0, 1):
        put(b, 0, first_ref[:, b, :N, :] + from_left[:, b, :N, :] * has_left + from_above[:, b] * has_above)
    for copy in started:
        copy.wait_send()


def exchange(first, second, object_field, total, probe):
    vmem = pl.BlockSpec(memory_space=pltpu.VMEM)
    f32 = jnp.float32
    dma = pltpu.SemaphoreType.DMA
    return pl.pallas_call(
        exchange_kernel,
        out_shape=(
            jax.ShapeDtypeStruct((2, BLOCK, BLOCK), f32),
            jax.ShapeDtypeStruct((2, N, N), f32),
        ),
        in_specs=[vmem] * 5,
        out_specs=(vmem, vmem),
        scratch_shapes=[
            pltpu.VMEM((2, 2, WIDE, H), f32),
            pltpu.VMEM((2, 4, N, H), f32),
            pltpu.VMEM((2, 2, N, H), f32),
            pltpu.VMEM((N, N), f32),
            pltpu.VMEM((N, N), f32),
            pltpu.VMEM((3, 64, N), f32),
            pltpu.VMEM((16, 8, H), f32),
            pltpu.VMEM((15, 8, H), f32),
            pltpu.VMEM((2, 4, 16, 8, H), f32),
            dma((3,)), dma((3,)), dma((2,)), dma((2,)), dma((1,)), dma((1,)), dma((3,)), dma((3,)),
            dma((15,)), dma((15,)), dma((15,)), dma((15,)), dma((3,)), dma((3,)), dma((4,)), dma((4,)),
        ],
        compiler_params=pltpu.CompilerParams(
            collective_id=0, has_side_effects=True, vmem_limit_bytes=32 * 1024 * 1024
        ),
    )(first, second, object_field, total, probe)


def shards(object_field, probe, amplitudes, corner_rows, corner_cols, counts):
    tables = [jnp.asarray(t) for t in stage_tables()]
    lower = passed_along(object_field[:, :N, :], "tile", -1)
    right = passed_along(object_field[:, :, :N], "pos", -1)
    corner = passed_along(lower[:, :, :N], "pos", -1)
    scalars = (corner_rows, corner_cols, counts)
    upd1, sum1 = run_slots(
        lambda r, c: r <= BLOCK - N, 0, BLOCK, ((0, 0), (0, BLOCK)), (object_field, right), (),
        scalars, probe, amplitudes, tables,
    )
    upd2, sum2 = run_slots(
        lambda r, c: r > BLOCK - N, N, BLOCK, ((0, 0), (0, BLOCK), (N, 0), (N, BLOCK)),
        (object_field[:, N:, :], right[:, N:, :], lower, corner), (upd1, sum1),
        scalars, probe, amplitudes, tables,
    )
    return exchange(upd1, upd2, object_field, sum2.reshape(2 * N, N), probe)


def solution(mesh):
    return jax.shard_map(
        shards,
        mesh=mesh,
        in_specs=(
            P(None, "tile", "pos"),
            P(),
            P("tile", "pos", None, None, None),
            P("tile", "pos", None),
            P("tile", "pos", None),
            P("tile", "pos"),
        ),
        out_specs=(P(None, "tile", "pos"), P()),
        check_vma=False,
    )
```

```python
import functools
import math

import jax
import jax.numpy as jnp
import ml_dtypes
import numpy as np
from jax import lax
from jax.experimental import pallas as pl
from jax.experimental.pallas import tpu as pltpu
from jax.sharding import PartitionSpec as P

N = 256
H = 128
BLOCK = 512
WIDE = 768
LIMIT = 24 * 1024 * 1024


def dft_tables():
    j = np.arange(N)
    angle = (j[:, None] * j[None, :] % N) * (2.0 * np.pi / N)
    re = (np.cos(angle) / np.sqrt(N)).astype(np.float32).astype(ml_dtypes.bfloat16)
    im = (-np.sin(angle) / np.sqrt(N)).astype(np.float32).astype(ml_dtypes.bfloat16)
    return re, im


def stage_tables():
    re, im = dft_tables()

    def pair(a, b, c, d):
        return np.concatenate([np.concatenate([a, b], 1), np.concatenate([c, d], 1)], 0)

    first = [pair(re[:H, q::2], -im[:H, q::2], im[:H, q::2], re[:H, q::2]) for q in (0, 1)]
    second = pair(re, im, -im, re)
    third = [pair(re[q::2, :H], im[q::2, :H], -im[q::2, :H], re[q::2, :H]) for q in (0, 1)]
    fourth = pair(re, -im, im, re)
    return np.stack(first), second, np.stack(third), fourth


def slots_kernel(
    rule, places, first, last,
    rows_ref, cols_ref, count_ref, amp_ref, t1_ref, t2_ref, t3_ref, t4_ref, *refs,
):
    n_pieces = len(places)
    pieces = refs[:n_pieces]
    refs = refs[n_pieces:]
    if first:
        probe_ref = refs[0]
    refs = refs[1 if first else 4 :]
    ext, upd_ref, psum_ref, prb = refs[:4]
    (pat, ext_b, exit_s, near_b, fold_b, back_b, amp_buf, lanes_buf, order, piece_sem, amp_sem) = refs[4:]
    copies = []

    def bring(source, target):
        copies.append(pltpu.make_async_copy(source, target, piece_sem.at[len(copies)]))
        copies[-1].start()

    for piece, (r0, c0) in zip(pieces, places):
        _, h, w = piece.shape
        for b in range(w // H):
            bring(piece.at[:, :, b * H : (b + 1) * H], ext.at[:, c0 // H + b, r0 : r0 + h, :])

    def collect(s, n):
        order[n] = s
        keep = jnp.logical_and(s < count_ref[0, 0], rule(rows_ref[0, 0, s], cols_ref[0, 0, s]))
        return n + keep.astype(jnp.int32)

    total = lax.fori_loop(0, rows_ref.shape[2], collect, jnp.int32(0))

    def amp_copy(i):
        slot = lax.rem(i, 2)
        return pltpu.make_async_copy(amp_ref.at[0, 0, order[i]], amp_buf.at[slot], amp_sem.at[slot])

    @pl.when(total > 0)
    def _():
        amp_copy(0).start()

    if first:
        for b in range(2):
            bring(probe_ref.at[:, :, b * H : (b + 1) * H], lanes_buf.at[:, b])
        upd_ref[...] = jnp.zeros_like(upd_ref)
        psum_ref[...] = jnp.zeros_like(psum_ref)
    for copy in copies:
        copy.wait()
    if first:
        for comp in range(2):
            for q in range(2):
                for b in range(2):
                    prb[comp, q * H : (q + 1) * H, b * H : (b + 1) * H] = lanes_buf[comp, b, pl.ds(q, H, stride=2), :]

    lane = lax.broadcasted_iota(jnp.int32, (H, H), 1)

    def step(i, carry):
        s = order[i]
        r = rows_ref[0, 0, s]
        c = cols_ref[0, 0, s]
        off = lax.rem(c, H)
        c0 = c // H
        back_shift = lax.rem(H - off, H)

        @pl.when(i + 1 < total)
        def _():
            amp_copy(i + 1).start()

        for q in range(2):
            part = []
            for comp in range(2):
                blocks = [
                    pltpu.roll(ext[comp, c0 + b, pl.ds(r + q, H, stride=2), :], back_shift, 1)
                    for b in range(3)
                ]
                part.append(
                    [jnp.where(lane < H - off, blocks[b], blocks[b + 1]) for b in range(2)]
                )
            for b in range(2):
                here = (slice(q * H, (q + 1) * H), slice(b * H, (b + 1) * H))
                pre, pim = prb[0][here], prb[1][here]
                are, aim = part[0][b], part[1][b]
                ere = pre * are - pim * aim
                eim = pre * aim + pim * are
                pat[(0,) + here] = are
                pat[(1,) + here] = aim
                exit_s[(0,) + here] = ere
                exit_s[(1,) + here] = eim
                ext_b[q, 0:H, b * H : (b + 1) * H] = ere.astype(jnp.bfloat16)
                ext_b[q, H:N, b * H : (b + 1) * H] = eim.astype(jnp.bfloat16)

        dot = functools.partial(jnp.dot, preferred_element_type=jnp.float32)
        even = dot(t1_ref[0], ext_b[0])
        odd = dot(t1_ref[1], ext_b[1])
        for comp in range(2):
            e, o = even[comp * H : (comp + 1) * H], odd[comp * H : (comp + 1) * H]
            near_b[0:H, comp * N : (comp + 1) * N] = (e + o).astype(jnp.bfloat16)
            near_b[H:N, comp * N : (comp + 1) * N] = (e - o).astype(jnp.bfloat16)

        amp_copy(i).wait()
        amp = amp_buf.at[lax.rem(i, 2)]
        far = dot(near_b[...], t2_ref[...])
        fre, fim = far[:, :N], far[:, N:]
        ratio = amp[...].astype(jnp.float32) * lax.rsqrt(fre * fre + fim * fim + 0.25)
        for comp, part in enumerate((fre * ratio, fim * ratio)):
            top, low = part[:H], part[H:]
            fold_b[0, comp * H : (comp + 1) * H, :] = (top + low).astype(jnp.bfloat16)
            fold_b[1, comp * H : (comp + 1) * H, :] = (top - low).astype(jnp.bfloat16)

        for q in range(2):
            back = dot(t3_ref[q], fold_b[q])
            for comp in range(2):
                back_b[q * H : (q + 1) * H, comp * N : (comp + 1) * N] = back[comp * H : (comp + 1) * H].astype(
                    jnp.bfloat16
                )
        new = dot(back_b[...], t4_ref[...])
        dre = new[:, :N] - exit_s[0]
        dim = new[:, N:] - exit_s[1]
        psum_ref[0] += pat[0] * dre + pat[1] * dim
        psum_ref[1] += pat[0] * dim - pat[1] * dre
        terms = (prb[0] * dre + prb[1] * dim, prb[0] * dim - prb[1] * dre)
        for comp in range(2):
            for q in range(2):
                z0 = pltpu.roll(terms[comp][q * H : (q + 1) * H, :H], off, 1)
                z1 = pltpu.roll(terms[comp][q * H : (q + 1) * H, H:], off, 1)
                zero = jnp.zeros_like(z0)
                for b, val in enumerate(
                    (jnp.where(lane >= off, z0, zero), jnp.where(lane >= off, z1, z0), jnp.where(lane >= off, zero, z1))
                ):
                    here = (comp, c0 + b, pl.ds(r + q, H, stride=2), slice(None))
                    upd_ref[here] = upd_ref[here] + val
        return carry

    lax.fori_loop(0, total, step, 0)
    if last:
        for comp in range(2):
            for b in range(2):
                lanes = slice(b * H, (b + 1) * H)
                for q in range(2):
                    lanes_buf[comp, b, pl.ds(q, H, stride=2), :] = psum_ref[comp, q * H : (q + 1) * H, lanes]
                psum_ref[comp, :, lanes] = lanes_buf[comp, b]


def run_slots(rule, places, pieces, state, last, scalars, amplitudes, tables):
    smem = pl.BlockSpec(memory_space=pltpu.SMEM)
    vmem = pl.BlockSpec(memory_space=pltpu.VMEM)
    hbm = pl.BlockSpec(memory_space=pl.ANY)
    first = len(state) == 1
    shapes = [(2, WIDE // H, WIDE, H)] * 2 + [(2, N, N)] * 2
    at = 8 + len(pieces)
    return pl.pallas_call(
        functools.partial(slots_kernel, rule, places, first, last),
        out_shape=tuple(jax.ShapeDtypeStruct(shape, jnp.float32) for shape in shapes),
        in_specs=[smem] * 3 + [hbm] + [vmem] * 4 + [hbm] * len(pieces) + ([hbm] if first else [vmem] * 4),
        out_specs=(vmem,) * 4,
        input_output_aliases={} if first else {at + i: i for i in range(4)},
        scratch_shapes=[
            pltpu.VMEM((2, N, N), jnp.float32),
            pltpu.VMEM((2, N, N), jnp.bfloat16),
            pltpu.VMEM((2, N, N), jnp.float32),
            pltpu.VMEM((N, 2 * N), jnp.bfloat16),
            pltpu.VMEM((2, N, N), jnp.bfloat16),
            pltpu.VMEM((N, 2 * N), jnp.bfloat16),
            pltpu.VMEM((2, N, N), jnp.bfloat16),
            pltpu.VMEM((2, 2, N, H), jnp.float32),
            pltpu.SMEM((40,), jnp.int32),
            pltpu.SemaphoreType.DMA((2 + sum(p.shape[2] // H for p in pieces),)),
            pltpu.SemaphoreType.DMA((2,)),
        ],
        compiler_params=pltpu.CompilerParams(vmem_limit_bytes=LIMIT),
        cost_estimate=pl.CostEstimate(flops=10_000_000_000, bytes_accessed=4_000_000, transcendentals=0),
    )(*scalars, amplitudes, *tables, *pieces, *state)


def passed_along(block, axis, distance):
    devices = range(lax.axis_size(axis))
    route = [(i - distance, i) for i in devices if i - distance in devices]
    return lax.ppermute(block, axis, route)


def exchange_kernel(
    upd_ref, obj_ref, sum_ref, probe_ref, out_ref, grad_ref,
    from_left, from_above, corner, pair_in, part, x_in, piece, tile_in, gathered,
    right_send, right_recv, low_send, low_recv, pair_send, pair_recv, x_send, x_recv,
    t_send, t_recv, tg_send, tg_recv, xg_send, xg_recv, cg_send, cg_recv,
):
    p = lax.axis_index("pos")
    t = lax.axis_index("tile")
    x, z, core = p // 8, (p // 2) % 4, p % 2
    g = z * 4 + t

    def pos_of(xx, zz, cc):
        return xx * 8 + zz * 2 + cc

    right = {"pos": (p + 1) % 32, "tile": t}
    left = {"pos": (p + 31) % 32, "tile": t}
    below = {"pos": p, "tile": (t + 1) % 4}
    partner = {"pos": pos_of(x, z, 1 - core), "tile": t}
    x_peers = [{"pos": pos_of((x + d) % 4, z, core), "tile": t} for d in (1, 2, 3)]
    g_peers = [{"pos": pos_of(x, ((g + d) % 16) // 4, core), "tile": (g + d) % 4} for d in range(1, 16)]

    barrier = pltpu.get_barrier_semaphore()
    for peer in [right, left, partner] + x_peers + g_peers:
        pl.semaphore_signal(barrier, inc=1, device_id=peer, device_id_type=pl.DeviceIdType.MESH)
    pl.semaphore_wait(barrier, 21)

    started = []

    def send(source, target, send_sem, recv_sem, peer):
        copy = pltpu.make_async_remote_copy(
            src_ref=source, dst_ref=target, send_sem=send_sem, recv_sem=recv_sem,
            device_id=peer, device_id_type=pl.DeviceIdType.MESH,
        )
        copy.start()
        started.append(copy)
        return copy

    edge = send(upd_ref.at[:, 4:6, 2 * N :, :], from_left.at[:, :, 2 * N :, :], right_send.at[0], right_recv.at[0], right)
    low1 = send(upd_ref.at[:, 2:4, 2 * N :, :], from_above.at[:, 2:4], low_send.at[0], low_recv.at[0], below)
    half = send(sum_ref.at[pl.ds((1 - core) * N, N)], pair_in, pair_send.at[0], pair_recv.at[0], partner)
    mid = send(upd_ref.at[:, 4:6, N : 2 * N, :], from_left.at[:, :, N : 2 * N, :], right_send.at[1], right_recv.at[1], right)

    half.wait_recv()
    part[...] = sum_ref[pl.ds(core * N, N), :] + pair_in[...]
    x_copies = [
        send(part.at[pl.ds(((x + d) % 4) * 64, 64)], x_in.at[d - 1], x_send.at[d - 1], x_recv.at[d - 1], x_peers[d - 1])
        for d in (1, 2, 3)
    ]

    edge.wait_recv()
    has_left = (p > 0).astype(jnp.float32)
    has_above = (t > 0).astype(jnp.float32)
    corner[...] = upd_ref[:, 0:2, 2 * N :, :] + from_left[:, :, 2 * N :, :] * has_left

    for copy in x_copies:
        copy.wait_recv()
    shard = part[pl.ds(x * 64, 64), :] + x_in[0] + x_in[1] + x_in[2]
    for rg in range(8):
        for lg in range(2):
            piece[rg * 2 + lg] = shard[rg * 8 : rg * 8 + 8, lg * H : (lg + 1) * H]
    t_copies = [
        send(piece.at[(g + d) % 16], tile_in.at[d - 1], t_send.at[d - 1], t_recv.at[d - 1], g_peers[d - 1])
        for d in range(1, 16)
    ]
    low0a = send(corner.at[:, 0], from_above.at[:, 0], low_send.at[1], low_recv.at[1], below)
    power = jnp.sum(probe_ref[...] * probe_ref[...]) * (1.0 / (N * N)) + 1e-06
    scale = 1.0 / jnp.full((1, H), power, jnp.float32)

    for copy in t_copies:
        copy.wait_recv()
    own = piece[g]
    for d in range(15):
        own = own + tile_in[d]
    slots = 128 * 32
    gathered[core, x, g] = own * np.float32(1.0 / math.sqrt(slots))
    tg_copies = [
        send(gathered.at[core, x, g], gathered.at[core, x, g], tg_send.at[d - 1], tg_recv.at[d - 1], g_peers[d - 1])
        for d in range(1, 16)
    ]

    low0b = send(corner.at[:, 1], from_above.at[:, 1], low_send.at[2], low_recv.at[2], below)
    top = send(upd_ref.at[:, 4:6, :N, :], from_left.at[:, :, :N, :], right_send.at[2], right_recv.at[2], right)

    for copy in tg_copies:
        copy.wait_recv()
    xg_copies = [
        send(gathered.at[core, x], gathered.at[core, x], xg_send.at[d - 1], xg_recv.at[d - 1], x_peers[d - 1])
        for d in (1, 2, 3)
    ]
    cg_copies = [send(gathered.at[core, x], gathered.at[core, x], cg_send.at[0], cg_recv.at[0], partner)]

    def put(b, r0, value):
        for comp in range(2):
            here = (comp, slice(r0, r0 + N), slice(b * H, (b + 1) * H))
            out_ref[here] = obj_ref[here] + value[comp] * scale

    for b in (2, 3):
        put(b, N, upd_ref[:, b, N : 2 * N, :])
    for d in (1, 2, 3):
        xg_copies[d - 1].wait_recv()
        came = (x + 4 - d) % 4
        cg_copies.append(
            send(gathered.at[core, came], gathered.at[core, came], cg_send.at[d], cg_recv.at[d], partner)
        )
    mid.wait_recv()
    for b in (0, 1):
        put(b, N, upd_ref[:, b, N : 2 * N, :] + from_left[:, b, N : 2 * N, :] * has_left)
    low1.wait_recv()
    for b in (2, 3):
        put(b, 0, upd_ref[:, b, :N, :] + from_above[:, b] * has_above)
    top.wait_recv()
    for copy in cg_copies:
        copy.wait_recv()
    for h in range(2):
        for xx in range(4):
            for rg in range(8):
                for lg in range(2):
                    grad_ref[h, xx * 64 + rg * 8 : xx * 64 + rg * 8 + 8, lg * H : (lg + 1) * H] = gathered[h, xx, rg * 2 + lg]
    low0a.wait_recv()
    low0b.wait_recv()
    for b in (0, 1):
        put(b, 0, upd_ref[:, b, :N, :] + from_left[:, b, :N, :] * has_left + from_above[:, b] * has_above)
    for copy in started:
        copy.wait_send()


def exchange(update, object_field, total, probe):
    vmem = pl.BlockSpec(memory_space=pltpu.VMEM)
    f32 = jnp.float32
    dma = pltpu.SemaphoreType.DMA
    return pl.pallas_call(
        exchange_kernel,
        out_shape=(
            jax.ShapeDtypeStruct((2, BLOCK, BLOCK), f32),
            jax.ShapeDtypeStruct((2, N, N), f32),
        ),
        in_specs=[vmem] * 4,
        out_specs=(vmem, vmem),
        scratch_shapes=[
            pltpu.VMEM((2, 2, WIDE, H), f32),
            pltpu.VMEM((2, 4, N, H), f32),
            pltpu.VMEM((2, 2, N, H), f32),
            pltpu.VMEM((N, N), f32),
            pltpu.VMEM((N, N), f32),
            pltpu.VMEM((3, 64, N), f32),
            pltpu.VMEM((16, 8, H), f32),
            pltpu.VMEM((15, 8, H), f32),
            pltpu.VMEM((2, 4, 16, 8, H), f32),
            dma((3,)), dma((3,)), dma((3,)), dma((3,)), dma((1,)), dma((1,)), dma((3,)), dma((3,)),
            dma((15,)), dma((15,)), dma((15,)), dma((15,)), dma((3,)), dma((3,)), dma((4,)), dma((4,)),
        ],
        compiler_params=pltpu.CompilerParams(
            collective_id=0, has_side_effects=True, vmem_limit_bytes=32 * 1024 * 1024
        ),
    )(update, object_field, total, probe)


def shards(object_field, probe, amplitudes, corner_rows, corner_cols, counts):
    tables = [jnp.asarray(t) for t in stage_tables()]
    low_a = passed_along(object_field[:, :N, :N], "tile", -1)
    right = passed_along(object_field[:, :, :N], "pos", -1)
    low_b = passed_along(object_field[:, :N, N:], "tile", -1)
    corner = passed_along(low_a, "pos", -1)
    fixed = ((corner_rows, corner_cols, counts), amplitudes, tables)
    reach = BLOCK - N
    state = run_slots(
        lambda r, c: (r <= reach) & (c <= reach), ((0, 0),), (object_field,), (probe,), False, *fixed
    )
    state = run_slots(lambda r, c: (r <= reach) & (c > reach), ((0, BLOCK),), (right,), state, False, *fixed)
    _, update, total, _ = run_slots(
        lambda r, c: r > reach, ((BLOCK, 0), (BLOCK, N), (BLOCK, BLOCK)), (low_a, low_b, corner), state, True, *fixed
    )
    return exchange(update, object_field, total.reshape(2 * N, N), probe)


def solution(mesh):
    return jax.shard_map(
        shards,
        mesh=mesh,
        in_specs=(
            P(None, "tile", "pos"),
            P(),
            P("tile", "pos", None, None, None),
            P("tile", "pos", None),
            P("tile", "pos", None),
            P("tile", "pos"),
        ),
        out_specs=(P(None, "tile", "pos"), P()),
        check_vma=False,
    )
```

```python
import functools
import math

import jax
import jax.numpy as jnp
import ml_dtypes
import numpy as np
from jax import lax
from jax.experimental import pallas as pl
from jax.experimental.pallas import tpu as pltpu
from jax.sharding import PartitionSpec as P

N = 256
H = 128
BLOCK = 512
WIDE = 768
LIMIT = 24 * 1024 * 1024


def dft_tables():
    j = np.arange(N)
    angle = (j[:, None] * j[None, :] % N) * (2.0 * np.pi / N)
    re = (np.cos(angle) / np.sqrt(N)).astype(np.float32).astype(ml_dtypes.bfloat16)
    im = (-np.sin(angle) / np.sqrt(N)).astype(np.float32).astype(ml_dtypes.bfloat16)
    return re, im


def stage_tables():
    re, im = dft_tables()

    def pair(a, b, c, d):
        return np.concatenate([np.concatenate([a, b], 1), np.concatenate([c, d], 1)], 0)

    first = [pair(re[:H, q::2], -im[:H, q::2], im[:H, q::2], re[:H, q::2]) for q in (0, 1)]
    second = pair(re, im, -im, re)
    third = [pair(re[q::2, :H], im[q::2, :H], -im[q::2, :H], re[q::2, :H]) for q in (0, 1)]
    fourth = pair(re, -im, im, re)
    return np.stack(first), second, np.stack(third), fourth


def slots_kernel(
    rule, places, first, last,
    rows_ref, cols_ref, count_ref, amp_ref, t1_ref, t2_ref, t3_ref, t4_ref, *refs,
):
    n_pieces = len(places)
    pieces = refs[:n_pieces]
    refs = refs[n_pieces:]
    if first:
        probe_ref = refs[0]
    refs = refs[1 if first else 4 :]
    ext, upd_ref, psum_ref, prb = refs[:4]
    (pat, ext_b, exit_s, near_b, fold_b, back_b, amp_buf, lanes_buf, order, piece_sem, amp_sem) = refs[4:]
    copies = []

    def bring(source, target):
        copies.append(pltpu.make_async_copy(source, target, piece_sem.at[len(copies)]))
        copies[-1].start()

    for piece, (r0, c0) in zip(pieces, places):
        _, h, w = piece.shape
        for b in range(w // H):
            bring(piece.at[:, :, b * H : (b + 1) * H], ext.at[:, c0 // H + b, r0 : r0 + h, :])

    def collect(s, n):
        order[n] = s
        keep = jnp.logical_and(s < count_ref[0, 0], rule(rows_ref[0, 0, s], cols_ref[0, 0, s]))
        return n + keep.astype(jnp.int32)

    total = lax.fori_loop(0, rows_ref.shape[2], collect, jnp.int32(0))

    def amp_copy(i):
        slot = lax.rem(i, 2)
        return pltpu.make_async_copy(amp_ref.at[0, 0, order[i]], amp_buf.at[slot], amp_sem.at[slot])

    @pl.when(total > 0)
    def _():
        amp_copy(0).start()

    if first:
        for b in range(2):
            bring(probe_ref.at[:, :, b * H : (b + 1) * H], lanes_buf.at[:, b])
        upd_ref[...] = jnp.zeros_like(upd_ref)
        psum_ref[...] = jnp.zeros_like(psum_ref)
    for copy in copies:
        copy.wait()
    if first:
        for comp in range(2):
            for q in range(2):
                for b in range(2):
                    prb[comp, q * H : (q + 1) * H, b * H : (b + 1) * H] = lanes_buf[comp, b, pl.ds(q, H, stride=2), :]

    lane = lax.broadcasted_iota(jnp.int32, (H, H), 1)

    def step(i, carry):
        s = order[i]
        r = rows_ref[0, 0, s]
        c = cols_ref[0, 0, s]
        off = lax.rem(c, H)
        c0 = c // H
        back_shift = lax.rem(H - off, H)

        @pl.when(i + 1 < total)
        def _():
            amp_copy(i + 1).start()

        for q in range(2):
            part = []
            for comp in range(2):
                blocks = [
                    pltpu.roll(ext[comp, c0 + b, pl.ds(r + q, H, stride=2), :], back_shift, 1)
                    for b in range(3)
                ]
                part.append(
                    [jnp.where(lane < H - off, blocks[b], blocks[b + 1]) for b in range(2)]
                )
            for b in range(2):
                here = (slice(q * H, (q + 1) * H), slice(b * H, (b + 1) * H))
                pre, pim = prb[0][here], prb[1][here]
                are, aim = part[0][b], part[1][b]
                ere = pre * are - pim * aim
                eim = pre * aim + pim * are
                pat[(0,) + here] = are
                pat[(1,) + here] = aim
                exit_s[(0,) + here] = ere
                exit_s[(1,) + here] = eim
                ext_b[q, 0:H, b * H : (b + 1) * H] = ere.astype(jnp.bfloat16)
                ext_b[q, H:N, b * H : (b + 1) * H] = eim.astype(jnp.bfloat16)

        dot = functools.partial(jnp.dot, preferred_element_type=jnp.float32)
        even = dot(t1_ref[0], ext_b[0])
        odd = dot(t1_ref[1], ext_b[1])
        for comp in range(2):
            e, o = even[comp * H : (comp + 1) * H], odd[comp * H : (comp + 1) * H]
            near_b[0:H, comp * N : (comp + 1) * N] = (e + o).astype(jnp.bfloat16)
            near_b[H:N, comp * N : (comp + 1) * N] = (e - o).astype(jnp.bfloat16)

        amp_copy(i).wait()
        amp = amp_buf.at[lax.rem(i, 2)]
        far = dot(near_b[...], t2_ref[...])
        fre, fim = far[:, :N], far[:, N:]
        ratio = amp[...].astype(jnp.float32) * lax.rsqrt(fre * fre + fim * fim + 0.25)
        for comp, part in enumerate((fre * ratio, fim * ratio)):
            top, low = part[:H], part[H:]
            fold_b[0, comp * H : (comp + 1) * H, :] = (top + low).astype(jnp.bfloat16)
            fold_b[1, comp * H : (comp + 1) * H, :] = (top - low).astype(jnp.bfloat16)

        for q in range(2):
            back = dot(t3_ref[q], fold_b[q])
            for comp in range(2):
                back_b[q * H : (q + 1) * H, comp * N : (comp + 1) * N] = back[comp * H : (comp + 1) * H].astype(
                    jnp.bfloat16
                )
        new = dot(back_b[...], t4_ref[...])
        dre = new[:, :N] - exit_s[0]
        dim = new[:, N:] - exit_s[1]
        psum_ref[0] += pat[0] * dre + pat[1] * dim
        psum_ref[1] += pat[0] * dim - pat[1] * dre
        terms = (prb[0] * dre + prb[1] * dim, prb[0] * dim - prb[1] * dre)
        for comp in range(2):
            for q in range(2):
                z0 = pltpu.roll(terms[comp][q * H : (q + 1) * H, :H], off, 1)
                z1 = pltpu.roll(terms[comp][q * H : (q + 1) * H, H:], off, 1)
                zero = jnp.zeros_like(z0)
                for b, val in enumerate(
                    (jnp.where(lane >= off, z0, zero), jnp.where(lane >= off, z1, z0), jnp.where(lane >= off, zero, z1))
                ):
                    here = (comp, c0 + b, pl.ds(r + q, H, stride=2), slice(None))
                    upd_ref[here] = upd_ref[here] + val
        return carry

    lax.fori_loop(0, total, step, 0)
    if last:
        for comp in range(2):
            for b in range(2):
                lanes = slice(b * H, (b + 1) * H)
                for q in range(2):
                    lanes_buf[comp, b, pl.ds(q, H, stride=2), :] = psum_ref[comp, q * H : (q + 1) * H, lanes]
                psum_ref[comp, :, lanes] = lanes_buf[comp, b]


def run_slots(rule, places, pieces, state, last, scalars, amplitudes, tables):
    smem = pl.BlockSpec(memory_space=pltpu.SMEM)
    vmem = pl.BlockSpec(memory_space=pltpu.VMEM)
    hbm = pl.BlockSpec(memory_space=pl.ANY)
    far = pl.BlockSpec(memory_space=pltpu.HBM)
    first = len(state) == 1
    shapes = [(2, WIDE // H, WIDE, H)] * 2 + [(2, N, N)] * 2
    at = 8 + len(pieces)
    return pl.pallas_call(
        functools.partial(slots_kernel, rule, places, first, last),
        out_shape=tuple(jax.ShapeDtypeStruct(shape, jnp.float32) for shape in shapes),
        in_specs=[smem] * 3 + [far] + [vmem] * 4 + [hbm] * len(pieces) + ([hbm] if first else [vmem] * 4),
        out_specs=(vmem,) * 4,
        input_output_aliases={} if first else {at + i: i for i in range(4)},
        scratch_shapes=[
            pltpu.VMEM((2, N, N), jnp.float32),
            pltpu.VMEM((2, N, N), jnp.bfloat16),
            pltpu.VMEM((2, N, N), jnp.float32),
            pltpu.VMEM((N, 2 * N), jnp.bfloat16),
            pltpu.VMEM((2, N, N), jnp.bfloat16),
            pltpu.VMEM((N, 2 * N), jnp.bfloat16),
            pltpu.VMEM((2, N, N), jnp.bfloat16),
            pltpu.VMEM((2, 2, N, H), jnp.float32),
            pltpu.SMEM((40,), jnp.int32),
            pltpu.SemaphoreType.DMA((2 + sum(p.shape[2] // H for p in pieces),)),
            pltpu.SemaphoreType.DMA((2,)),
        ],
        compiler_params=pltpu.CompilerParams(vmem_limit_bytes=LIMIT),
        cost_estimate=pl.CostEstimate(flops=10_000_000_000, bytes_accessed=4_000_000, transcendentals=0),
    )(*scalars, amplitudes, *tables, *pieces, *state)


def passed_along(block, axis, distance):
    devices = range(lax.axis_size(axis))
    route = [(i - distance, i) for i in devices if i - distance in devices]
    return lax.ppermute(block, axis, route)


def exchange_kernel(
    upd_ref, obj_ref, sum_ref, probe_ref, out_ref, grad_ref,
    from_left, from_above, corner, pair_in, part, x_in, piece, tile_in, gathered,
    right_send, right_recv, low_send, low_recv, pair_send, pair_recv, x_send, x_recv,
    t_send, t_recv, tg_send, tg_recv, xg_send, xg_recv, cg_send, cg_recv,
):
    p = lax.axis_index("pos")
    t = lax.axis_index("tile")
    x, z, core = p // 8, (p // 2) % 4, p % 2
    g = z * 4 + t

    def pos_of(xx, zz, cc):
        return xx * 8 + zz * 2 + cc

    right = {"pos": (p + 1) % 32, "tile": t}
    left = {"pos": (p + 31) % 32, "tile": t}
    below = {"pos": p, "tile": (t + 1) % 4}
    partner = {"pos": pos_of(x, z, 1 - core), "tile": t}
    x_peers = [{"pos": pos_of((x + d) % 4, z, core), "tile": t} for d in (1, 2, 3)]
    g_peers = [{"pos": pos_of(x, ((g + d) % 16) // 4, core), "tile": (g + d) % 4} for d in range(1, 16)]

    barrier = pltpu.get_barrier_semaphore()
    for peer in [right, left, partner] + x_peers + g_peers:
        pl.semaphore_signal(barrier, inc=1, device_id=peer, device_id_type=pl.DeviceIdType.MESH)
    pl.semaphore_wait(barrier, 21)

    started = []

    def send(source, target, send_sem, recv_sem, peer):
        copy = pltpu.make_async_remote_copy(
            src_ref=source, dst_ref=target, send_sem=send_sem, recv_sem=recv_sem,
            device_id=peer, device_id_type=pl.DeviceIdType.MESH,
        )
        copy.start()
        started.append(copy)
        return copy

    edge = send(upd_ref.at[:, 4:6, 2 * N :, :], from_left.at[:, :, 2 * N :, :], right_send.at[0], right_recv.at[0], right)
    low1 = send(upd_ref.at[:, 2:4, 2 * N :, :], from_above.at[:, 2:4], low_send.at[0], low_recv.at[0], below)
    half = send(sum_ref.at[pl.ds((1 - core) * N, N)], pair_in, pair_send.at[0], pair_recv.at[0], partner)
    mid = send(upd_ref.at[:, 4:6, N : 2 * N, :], from_left.at[:, :, N : 2 * N, :], right_send.at[1], right_recv.at[1], right)

    half.wait_recv()
    part[...] = sum_ref[pl.ds(core * N, N), :] + pair_in[...]
    x_copies = [
        send(part.at[pl.ds(((x + d) % 4) * 64, 64)], x_in.at[d - 1], x_send.at[d - 1], x_recv.at[d - 1], x_peers[d - 1])
        for d in (1, 2, 3)
    ]

    edge.wait_recv()
    has_left = (p > 0).astype(jnp.float32)
    has_above = (t > 0).astype(jnp.float32)
    corner[...] = upd_ref[:, 0:2, 2 * N :, :] + from_left[:, :, 2 * N :, :] * has_left

    for copy in x_copies:
        copy.wait_recv()
    shard = part[pl.ds(x * 64, 64), :] + x_in[0] + x_in[1] + x_in[2]
    for rg in range(8):
        for lg in range(2):
            piece[rg * 2 + lg] = shard[rg * 8 : rg * 8 + 8, lg * H : (lg + 1) * H]
    t_copies = [
        send(piece.at[(g + d) % 16], tile_in.at[d - 1], t_send.at[d - 1], t_recv.at[d - 1], g_peers[d - 1])
        for d in range(1, 16)
    ]
    low0a = send(corner.at[:, 0], from_above.at[:, 0], low_send.at[1], low_recv.at[1], below)
    power = jnp.sum(probe_ref[...] * probe_ref[...]) * (1.0 / (N * N)) + 1e-06
    scale = 1.0 / jnp.full((1, H), power, jnp.float32)

    for copy in t_copies:
        copy.wait_recv()
    own = piece[g]
    for d in range(15):
        own = own + tile_in[d]
    slots = 128 * 32
    gathered[core, x, g] = own * np.float32(1.0 / math.sqrt(slots))
    tg_copies = [
        send(gathered.at[core, x, g], gathered.at[core, x, g], tg_send.at[d - 1], tg_recv.at[d - 1], g_peers[d - 1])
        for d in range(1, 16)
    ]

    low0b = send(corner.at[:, 1], from_above.at[:, 1], low_send.at[2], low_recv.at[2], below)
    top = send(upd_ref.at[:, 4:6, :N, :], from_left.at[:, :, :N, :], right_send.at[2], right_recv.at[2], right)

    for copy in tg_copies:
        copy.wait_recv()
    xg_copies = [
        send(gathered.at[core, x], gathered.at[core, x], xg_send.at[d - 1], xg_recv.at[d - 1], x_peers[d - 1])
        for d in (1, 2, 3)
    ]
    cg_copies = [send(gathered.at[core, x], gathered.at[core, x], cg_send.at[0], cg_recv.at[0], partner)]

    def put(b, r0, value):
        for comp in range(2):
            here = (comp, slice(r0, r0 + N), slice(b * H, (b + 1) * H))
            out_ref[here] = obj_ref[here] + value[comp] * scale

    for b in (2, 3):
        put(b, N, upd_ref[:, b, N : 2 * N, :])
    for d in (1, 2, 3):
        xg_copies[d - 1].wait_recv()
        came = (x + 4 - d) % 4
        cg_copies.append(
            send(gathered.at[core, came], gathered.at[core, came], cg_send.at[d], cg_recv.at[d], partner)
        )
    mid.wait_recv()
    for b in (0, 1):
        put(b, N, upd_ref[:, b, N : 2 * N, :] + from_left[:, b, N : 2 * N, :] * has_left)
    low1.wait_recv()
    for b in (2, 3):
        put(b, 0, upd_ref[:, b, :N, :] + from_above[:, b] * has_above)
    top.wait_recv()
    for copy in cg_copies:
        copy.wait_recv()
    for h in range(2):
        for xx in range(4):
            for rg in range(8):
                for lg in range(2):
                    grad_ref[h, xx * 64 + rg * 8 : xx * 64 + rg * 8 + 8, lg * H : (lg + 1) * H] = gathered[h, xx, rg * 2 + lg]
    low0a.wait_recv()
    low0b.wait_recv()
    for b in (0, 1):
        put(b, 0, upd_ref[:, b, :N, :] + from_left[:, b, :N, :] * has_left + from_above[:, b] * has_above)
    for copy in started:
        copy.wait_send()


def exchange(update, object_field, total, probe):
    vmem = pl.BlockSpec(memory_space=pltpu.VMEM)
    f32 = jnp.float32
    dma = pltpu.SemaphoreType.DMA
    return pl.pallas_call(
        exchange_kernel,
        out_shape=(
            jax.ShapeDtypeStruct((2, BLOCK, BLOCK), f32),
            jax.ShapeDtypeStruct((2, N, N), f32),
        ),
        in_specs=[vmem] * 4,
        out_specs=(vmem, vmem),
        scratch_shapes=[
            pltpu.VMEM((2, 2, WIDE, H), f32),
            pltpu.VMEM((2, 4, N, H), f32),
            pltpu.VMEM((2, 2, N, H), f32),
            pltpu.VMEM((N, N), f32),
            pltpu.VMEM((N, N), f32),
            pltpu.VMEM((3, 64, N), f32),
            pltpu.VMEM((16, 8, H), f32),
            pltpu.VMEM((15, 8, H), f32),
            pltpu.VMEM((2, 4, 16, 8, H), f32),
            dma((3,)), dma((3,)), dma((3,)), dma((3,)), dma((1,)), dma((1,)), dma((3,)), dma((3,)),
            dma((15,)), dma((15,)), dma((15,)), dma((15,)), dma((3,)), dma((3,)), dma((4,)), dma((4,)),
        ],
        compiler_params=pltpu.CompilerParams(
            collective_id=0, has_side_effects=True, vmem_limit_bytes=32 * 1024 * 1024
        ),
    )(update, object_field, total, probe)


def shards(object_field, probe, amplitudes, corner_rows, corner_cols, counts):
    tables = [jnp.asarray(t) for t in stage_tables()]
    low_a = passed_along(object_field[:, :N, :N], "tile", -1)
    corner = passed_along(low_a, "pos", -1)
    right = passed_along(object_field[:, :, :N], "pos", -1)
    low_b = passed_along(object_field[:, :N, N:], "tile", -1)
    fixed = ((corner_rows, corner_cols, counts), amplitudes, tables)
    reach = BLOCK - N
    state = run_slots(
        lambda r, c: r <= reach, ((0, 0), (0, BLOCK), (BLOCK, 0)), (object_field, right, low_a), (probe,), False, *fixed
    )
    _, update, total, _ = run_slots(
        lambda r, c: r > reach, ((BLOCK, N), (BLOCK, BLOCK)), (low_b, corner), state, True, *fixed
    )
    return exchange(update, object_field, total.reshape(2 * N, N), probe)


def solution(mesh):
    return jax.shard_map(
        shards,
        mesh=mesh,
        in_specs=(
            P(None, "tile", "pos"),
            P(),
            P("tile", "pos", None, None, None),
            P("tile", "pos", None),
            P("tile", "pos", None),
            P("tile", "pos"),
        ),
        out_specs=(P(None, "tile", "pos"), P()),
        check_vma=False,
    )
```

```python
import functools
import math

import jax
import jax.numpy as jnp
import ml_dtypes
import numpy as np
from jax import lax
from jax.experimental import pallas as pl
from jax.experimental.pallas import tpu as pltpu
from jax.sharding import PartitionSpec as P

N = 256
H = 128
BLOCK = 512
WIDE = 768
LIMIT = 24 * 1024 * 1024


def dft_tables():
    j = np.arange(N)
    angle = (j[:, None] * j[None, :] % N) * (2.0 * np.pi / N)
    re = (np.cos(angle) / np.sqrt(N)).astype(np.float32).astype(ml_dtypes.bfloat16)
    im = (-np.sin(angle) / np.sqrt(N)).astype(np.float32).astype(ml_dtypes.bfloat16)
    return re, im


def stage_tables():
    re, im = dft_tables()

    def pair(a, b, c, d):
        return np.concatenate([np.concatenate([a, b], 1), np.concatenate([c, d], 1)], 0)

    first = [pair(re[:H, q::2], -im[:H, q::2], im[:H, q::2], re[:H, q::2]) for q in (0, 1)]
    second = pair(re, im, -im, re)
    third = [pair(re[q::2, :H], im[q::2, :H], -im[q::2, :H], re[q::2, :H]) for q in (0, 1)]
    fourth = pair(re, -im, im, re)
    return np.stack(first), second, np.stack(third), fourth


def slots_kernel(
    rule, places, first, last,
    rows_ref, cols_ref, count_ref, amp_ref, t1_ref, t2_ref, t3_ref, t4_ref, *refs,
):
    n_pieces = len(places)
    pieces = refs[:n_pieces]
    refs = refs[n_pieces:]
    if first:
        probe_ref = refs[0]
    refs = refs[1 if first else 4 :]
    ext, upd_ref, psum_ref, prb = refs[:4]
    pat, ext_b, exit_s, amp_buf = (refs[4 + 4 * i : 8 + 4 * i] for i in range(4))
    near_b, fold_b, back_b, lanes_buf, order, piece_sem, amp_sem = refs[20:]
    copies = []

    def bring(source, target):
        copies.append(pltpu.make_async_copy(source, target, piece_sem.at[len(copies)]))
        copies[-1].start()

    for piece, (r0, c0) in zip(pieces, places):
        _, h, w = piece.shape
        for b in range(w // H):
            bring(piece.at[:, :, b * H : (b + 1) * H], ext.at[:, c0 // H + b, r0 : r0 + h, :])

    def collect(s, n):
        order[n] = s
        keep = jnp.logical_and(s < count_ref[0, 0], rule(rows_ref[0, 0, s], cols_ref[0, 0, s]))
        return n + keep.astype(jnp.int32)

    total = lax.fori_loop(0, rows_ref.shape[2], collect, jnp.int32(0))

    def amp_copy(i, k=0):
        return pltpu.make_async_copy(amp_ref.at[0, 0, order[i]], amp_buf[k], amp_sem.at[k])

    if first:
        for b in range(2):
            bring(probe_ref.at[:, :, b * H : (b + 1) * H], lanes_buf.at[:, b])
        upd_ref[...] = jnp.zeros_like(upd_ref)
        psum_ref[...] = jnp.zeros_like(psum_ref)
    for copy in copies:
        copy.wait()
    if first:
        for comp in range(2):
            for q in range(2):
                for b in range(2):
                    prb[comp, q * H : (q + 1) * H, b * H : (b + 1) * H] = lanes_buf[comp, b, pl.ds(q, H, stride=2), :]

    lane = lax.broadcasted_iota(jnp.int32, (H, H), 1)

    dot = functools.partial(jnp.dot, preferred_element_type=jnp.float32)

    def place(i):
        s = order[i]
        c = cols_ref[0, 0, s]
        return rows_ref[0, 0, s], c // H, lax.rem(c, H)

    def enter(i, k, q):
        r, c0, off = place(i)
        back_shift = lax.rem(H - off, H)
        keep = lane < H - off
        part = []
        for comp in range(2):
            blocks = [pltpu.roll(ext[comp, c0 + b, pl.ds(r + q, H, stride=2), :], back_shift, 1) for b in range(3)]
            part.append([jnp.where(keep, blocks[b], blocks[b + 1]) for b in range(2)])
        for b in range(2):
            here = (slice(q * H, (q + 1) * H), slice(b * H, (b + 1) * H))
            pre, pim = prb[(0,) + here], prb[(1,) + here]
            are, aim = part[0][b], part[1][b]
            ere = pre * are - pim * aim
            eim = pre * aim + pim * are
            pat[k][(0,) + here] = are
            pat[k][(1,) + here] = aim
            exit_s[k][(0,) + here] = ere
            exit_s[k][(1,) + here] = eim
            ext_b[k][q, 0:H, b * H : (b + 1) * H] = ere.astype(jnp.bfloat16)
            ext_b[k][q, H:N, b * H : (b + 1) * H] = eim.astype(jnp.bfloat16)

    def near(k, m):
        even = dot(t1_ref[0], ext_b[k][0])
        odd = dot(t1_ref[1], ext_b[k][1])
        for comp in range(2):
            e, o = even[comp * H : (comp + 1) * H], odd[comp * H : (comp + 1) * H]
            near_b[m, 0:H, comp * N : (comp + 1) * N] = (e + o).astype(jnp.bfloat16)
            near_b[m, H:N, comp * N : (comp + 1) * N] = (e - o).astype(jnp.bfloat16)

    def project(k, m):
        far = dot(near_b[m], t2_ref[...])
        fre, fim = far[:, :N], far[:, N:]
        ratio = amp_buf[k][...].astype(jnp.float32) * lax.rsqrt(fre * fre + fim * fim + 0.25)
        for comp, part in enumerate((fre * ratio, fim * ratio)):
            top, low = part[:H], part[H:]
            fold_b[m, 0, comp * H : (comp + 1) * H, :] = (top + low).astype(jnp.bfloat16)
            fold_b[m, 1, comp * H : (comp + 1) * H, :] = (top - low).astype(jnp.bfloat16)

    def back(k, m, q):
        part = dot(t3_ref[q], fold_b[m, q])
        for comp in range(2):
            back_b[m, q * H : (q + 1) * H, comp * N : (comp + 1) * N] = part[comp * H : (comp + 1) * H].astype(
                jnp.bfloat16
            )

    def finish(i, k, m, q, live):
        r, c0, off = place(i)
        here = slice(q * H, (q + 1) * H)
        new = dot(back_b[m, here], t4_ref[...])
        dre = new[:, :N] - exit_s[k][0, here]
        dim = new[:, N:] - exit_s[k][1, here]
        if live is not None:
            dre, dim = dre * live, dim * live
        psum_ref[0, here] += pat[k][0, here] * dre + pat[k][1, here] * dim
        psum_ref[1, here] += pat[k][0, here] * dim - pat[k][1, here] * dre
        pre, pim = prb[0, here], prb[1, here]
        terms = (pre * dre + pim * dim, pre * dim - pim * dre)
        for comp in range(2):
            z0 = pltpu.roll(terms[comp][:, :H], off, 1)
            z1 = pltpu.roll(terms[comp][:, H:], off, 1)
            zero = jnp.zeros_like(z0)
            keep = lane >= off
            for b, val in enumerate((jnp.where(keep, z0, zero), jnp.where(keep, z1, z0), jnp.where(keep, zero, z1))):
                spot = (comp, c0 + b, pl.ds(r + q, H, stride=2), slice(None))
                upd_ref[spot] = upd_ref[spot] + val

    final = jnp.maximum(total - 1, 0)
    pairs = (total + 1) // 2

    def fetch(pair, half):
        for m in range(2):
            amp_copy(jnp.minimum(2 * pair + m, final), 2 * half + m).start()

    def work(pair, half):
        follow = jnp.minimum(pair + 1, pairs - 1)
        ids = [jnp.minimum(2 * pair + m, final) for m in range(2)]
        nxt = [jnp.minimum(2 * follow + m, final) for m in range(2)]
        live = (2 * pair + 1 < total).astype(jnp.float32)
        for m in range(2):
            amp_copy(ids[m], 2 * half + m).wait()
        for m in range(2):
            near(2 * half + m, m)
        enter(nxt[0], 2 * (1 - half), 0)
        for m in range(2):
            project(2 * half + m, m)
        enter(nxt[0], 2 * (1 - half), 1)
        for m in range(2):
            for q in range(2):
                back(2 * half + m, m, q)
        enter(nxt[1], 2 * (1 - half) + 1, 0)
        for m in range(2):
            for q in range(2):
                finish(ids[m], 2 * half + m, m, q, live if m else None)
        enter(nxt[1], 2 * (1 - half) + 1, 1)

    @pl.when(total > 0)
    def _():
        fetch(0, 0)
        for m in range(2):
            for q in range(2):
                enter(jnp.minimum(m, final), m, q)

    def step(j, carry):
        for half in range(2):
            pair = 2 * j + half

            def run(pair=pair, half=half):
                @pl.when(pair + 1 < pairs)
                def _():
                    fetch(pair + 1, 1 - half)

                work(pair, half)

            if half == 0:
                run()
            else:
                pl.when(pair < pairs)(run)
        return carry

    lax.fori_loop(0, (pairs + 1) // 2, step, 0)
    if last:
        for comp in range(2):
            for b in range(2):
                lanes = slice(b * H, (b + 1) * H)
                for q in range(2):
                    lanes_buf[comp, b, pl.ds(q, H, stride=2), :] = psum_ref[comp, q * H : (q + 1) * H, lanes]
                psum_ref[comp, :, lanes] = lanes_buf[comp, b]


def run_slots(rule, places, pieces, state, last, scalars, amplitudes, tables):
    smem = pl.BlockSpec(memory_space=pltpu.SMEM)
    vmem = pl.BlockSpec(memory_space=pltpu.VMEM)
    hbm = pl.BlockSpec(memory_space=pl.ANY)
    far = pl.BlockSpec(memory_space=pltpu.HBM)
    first = len(state) == 1
    shapes = [(2, WIDE // H, WIDE, H)] * 2 + [(2, N, N)] * 2
    at = 8 + len(pieces)
    return pl.pallas_call(
        functools.partial(slots_kernel, rule, places, first, last),
        out_shape=tuple(jax.ShapeDtypeStruct(shape, jnp.float32) for shape in shapes),
        in_specs=[smem] * 3 + [far] + [vmem] * 4 + [hbm] * len(pieces) + ([hbm] if first else [vmem] * 4),
        out_specs=(vmem,) * 4,
        input_output_aliases={} if first else {at + i: i for i in range(4)},
        scratch_shapes=[
            *[pltpu.VMEM((2, N, N), jnp.float32)] * 4,
            *[pltpu.VMEM((2, N, N), jnp.bfloat16)] * 4,
            *[pltpu.VMEM((2, N, N), jnp.float32)] * 4,
            *[pltpu.VMEM((N, N), jnp.bfloat16)] * 4,
            pltpu.VMEM((2, N, 2 * N), jnp.bfloat16),
            pltpu.VMEM((2, 2, N, N), jnp.bfloat16),
            pltpu.VMEM((2, N, 2 * N), jnp.bfloat16),
            pltpu.VMEM((2, 2, N, H), jnp.float32),
            pltpu.SMEM((40,), jnp.int32),
            pltpu.SemaphoreType.DMA((2 + sum(p.shape[2] // H for p in pieces),)),
            pltpu.SemaphoreType.DMA((4,)),
        ],
        compiler_params=pltpu.CompilerParams(vmem_limit_bytes=LIMIT),
        cost_estimate=pl.CostEstimate(flops=10_000_000_000, bytes_accessed=4_000_000, transcendentals=0),
    )(*scalars, amplitudes, *tables, *pieces, *state)


def passed_along(block, axis, distance):
    devices = range(lax.axis_size(axis))
    route = [(i - distance, i) for i in devices if i - distance in devices]
    return lax.ppermute(block, axis, route)


def exchange_kernel(
    upd_ref, obj_ref, sum_ref, probe_ref, out_ref, grad_ref,
    from_left, from_above, corner, pair_in, part, x_in, piece, tile_in, gathered,
    right_send, right_recv, low_send, low_recv, pair_send, pair_recv, x_send, x_recv,
    t_send, t_recv, tg_send, tg_recv, xg_send, xg_recv, cg_send, cg_recv,
):
    p = lax.axis_index("pos")
    t = lax.axis_index("tile")
    x, z, core = p // 8, (p // 2) % 4, p % 2
    g = z * 4 + t

    def pos_of(xx, zz, cc):
        return xx * 8 + zz * 2 + cc

    right = {"pos": (p + 1) % 32, "tile": t}
    left = {"pos": (p + 31) % 32, "tile": t}
    below = {"pos": p, "tile": (t + 1) % 4}
    partner = {"pos": pos_of(x, z, 1 - core), "tile": t}
    x_peers = [{"pos": pos_of((x + d) % 4, z, core), "tile": t} for d in (1, 2, 3)]
    g_peers = [{"pos": pos_of(x, ((g + d) % 16) // 4, core), "tile": (g + d) % 4} for d in range(1, 16)]

    barrier = pltpu.get_barrier_semaphore()
    for peer in [right, left, partner] + x_peers + g_peers:
        pl.semaphore_signal(barrier, inc=1, device_id=peer, device_id_type=pl.DeviceIdType.MESH)
    pl.semaphore_wait(barrier, 21)

    started = []

    def send(source, target, send_sem, recv_sem, peer):
        copy = pltpu.make_async_remote_copy(
            src_ref=source, dst_ref=target, send_sem=send_sem, recv_sem=recv_sem,
            device_id=peer, device_id_type=pl.DeviceIdType.MESH,
        )
        copy.start()
        started.append(copy)
        return copy

    edge = send(upd_ref.at[:, 4:6, 2 * N :, :], from_left.at[:, :, 2 * N :, :], right_send.at[0], right_recv.at[0], right)
    low1 = send(upd_ref.at[:, 2:4, 2 * N :, :], from_above.at[:, 2:4], low_send.at[0], low_recv.at[0], below)
    half = send(sum_ref.at[pl.ds((1 - core) * N, N)], pair_in, pair_send.at[0], pair_recv.at[0], partner)
    mid = send(upd_ref.at[:, 4:6, N : 2 * N, :], from_left.at[:, :, N : 2 * N, :], right_send.at[1], right_recv.at[1], right)

    half.wait_recv()
    part[...] = sum_ref[pl.ds(core * N, N), :] + pair_in[...]
    x_copies = [
        send(part.at[pl.ds(((x + d) % 4) * 64, 64)], x_in.at[d - 1], x_send.at[d - 1], x_recv.at[d - 1], x_peers[d - 1])
        for d in (1, 2, 3)
    ]

    edge.wait_recv()
    has_left = (p > 0).astype(jnp.float32)
    has_above = (t > 0).astype(jnp.float32)
    corner[...] = upd_ref[:, 0:2, 2 * N :, :] + from_left[:, :, 2 * N :, :] * has_left

    for copy in x_copies:
        copy.wait_recv()
    shard = part[pl.ds(x * 64, 64), :] + x_in[0] + x_in[1] + x_in[2]
    for rg in range(8):
        for lg in range(2):
            piece[rg * 2 + lg] = shard[rg * 8 : rg * 8 + 8, lg * H : (lg + 1) * H]
    t_copies = [
        send(piece.at[(g + d) % 16], tile_in.at[d - 1], t_send.at[d - 1], t_recv.at[d - 1], g_peers[d - 1])
        for d in range(1, 16)
    ]
    low0a = send(corner.at[:, 0], from_above.at[:, 0], low_send.at[1], low_recv.at[1], below)
    power = jnp.sum(probe_ref[...] * probe_ref[...]) * (1.0 / (N * N)) + 1e-06
    scale = 1.0 / jnp.full((1, H), power, jnp.float32)

    for copy in t_copies:
        copy.wait_recv()
    own = piece[g]
    for d in range(15):
        own = own + tile_in[d]
    slots = 128 * 32
    gathered[core, x, g] = own * np.float32(1.0 / math.sqrt(slots))
    tg_copies = [
        send(gathered.at[core, x, g], gathered.at[core, x, g], tg_send.at[d - 1], tg_recv.at[d - 1], g_peers[d - 1])
        for d in range(1, 16)
    ]

    low0b = send(corner.at[:, 1], from_above.at[:, 1], low_send.at[2], low_recv.at[2], below)
    top = send(upd_ref.at[:, 4:6, :N, :], from_left.at[:, :, :N, :], right_send.at[2], right_recv.at[2], right)

    for copy in tg_copies:
        copy.wait_recv()
    xg_copies = [
        send(gathered.at[core, x], gathered.at[core, x], xg_send.at[d - 1], xg_recv.at[d - 1], x_peers[d - 1])
        for d in (1, 2, 3)
    ]
    cg_copies = [send(gathered.at[core, x], gathered.at[core, x], cg_send.at[0], cg_recv.at[0], partner)]

    def put(b, r0, value):
        for comp in range(2):
            here = (comp, slice(r0, r0 + N), slice(b * H, (b + 1) * H))
            out_ref[here] = obj_ref[here] + value[comp] * scale

    for b in (2, 3):
        put(b, N, upd_ref[:, b, N : 2 * N, :])
    for d in (1, 2, 3):
        xg_copies[d - 1].wait_recv()
        came = (x + 4 - d) % 4
        cg_copies.append(
            send(gathered.at[core, came], gathered.at[core, came], cg_send.at[d], cg_recv.at[d], partner)
        )
    mid.wait_recv()
    for b in (0, 1):
        put(b, N, upd_ref[:, b, N : 2 * N, :] + from_left[:, b, N : 2 * N, :] * has_left)
    low1.wait_recv()
    for b in (2, 3):
        put(b, 0, upd_ref[:, b, :N, :] + from_above[:, b] * has_above)
    top.wait_recv()
    for copy in cg_copies:
        copy.wait_recv()
    for h in range(2):
        for xx in range(4):
            for rg in range(8):
                for lg in range(2):
                    grad_ref[h, xx * 64 + rg * 8 : xx * 64 + rg * 8 + 8, lg * H : (lg + 1) * H] = gathered[h, xx, rg * 2 + lg]
    low0a.wait_recv()
    low0b.wait_recv()
    for b in (0, 1):
        put(b, 0, upd_ref[:, b, :N, :] + from_left[:, b, :N, :] * has_left + from_above[:, b] * has_above)
    for copy in started:
        copy.wait_send()


def exchange(update, object_field, total, probe):
    vmem = pl.BlockSpec(memory_space=pltpu.VMEM)
    f32 = jnp.float32
    dma = pltpu.SemaphoreType.DMA
    return pl.pallas_call(
        exchange_kernel,
        out_shape=(
            jax.ShapeDtypeStruct((2, BLOCK, BLOCK), f32),
            jax.ShapeDtypeStruct((2, N, N), f32),
        ),
        in_specs=[vmem] * 4,
        out_specs=(vmem, vmem),
        scratch_shapes=[
            pltpu.VMEM((2, 2, WIDE, H), f32),
            pltpu.VMEM((2, 4, N, H), f32),
            pltpu.VMEM((2, 2, N, H), f32),
            pltpu.VMEM((N, N), f32),
            pltpu.VMEM((N, N), f32),
            pltpu.VMEM((3, 64, N), f32),
            pltpu.VMEM((16, 8, H), f32),
            pltpu.VMEM((15, 8, H), f32),
            pltpu.VMEM((2, 4, 16, 8, H), f32),
            dma((3,)), dma((3,)), dma((3,)), dma((3,)), dma((1,)), dma((1,)), dma((3,)), dma((3,)),
            dma((15,)), dma((15,)), dma((15,)), dma((15,)), dma((3,)), dma((3,)), dma((4,)), dma((4,)),
        ],
        compiler_params=pltpu.CompilerParams(
            collective_id=0, has_side_effects=True, vmem_limit_bytes=32 * 1024 * 1024
        ),
    )(update, object_field, total, probe)


def shards(object_field, probe, amplitudes, corner_rows, corner_cols, counts):
    tables = [jnp.asarray(t) for t in stage_tables()]
    low_a = passed_along(object_field[:, :N, :N], "tile", -1)
    corner = passed_along(low_a, "pos", -1)
    right = passed_along(object_field[:, :, :N], "pos", -1)
    low_b = passed_along(object_field[:, :N, N:], "tile", -1)
    fixed = ((corner_rows, corner_cols, counts), amplitudes, tables)
    reach = BLOCK - N
    state = run_slots(
        lambda r, c: r <= reach, ((0, 0), (0, BLOCK), (BLOCK, 0)), (object_field, right, low_a), (probe,), False, *fixed
    )
    _, update, total, _ = run_slots(
        lambda r, c: r > reach, ((BLOCK, N), (BLOCK, BLOCK)), (low_b, corner), state, True, *fixed
    )
    return exchange(update, object_field, total.reshape(2 * N, N), probe)


def solution(mesh):
    return jax.shard_map(
        shards,
        mesh=mesh,
        in_specs=(
            P(None, "tile", "pos"),
            P(),
            P("tile", "pos", None, None, None),
            P("tile", "pos", None),
            P("tile", "pos", None),
            P("tile", "pos"),
        ),
        out_specs=(P(None, "tile", "pos"), P()),
        check_vma=False,
    )
```

```python
import functools
import math

import jax
import jax.numpy as jnp
import ml_dtypes
import numpy as np
from jax import lax
from jax.experimental import pallas as pl
from jax.experimental.pallas import tpu as pltpu
from jax.sharding import PartitionSpec as P

N = 256
H = 128
BLOCK = 512
WIDE = 768
LIMIT = 24 * 1024 * 1024


def dft_tables():
    j = np.arange(N)
    angle = (j[:, None] * j[None, :] % N) * (2.0 * np.pi / N)
    re = (np.cos(angle) / np.sqrt(N)).astype(np.float32).astype(ml_dtypes.bfloat16)
    im = (-np.sin(angle) / np.sqrt(N)).astype(np.float32).astype(ml_dtypes.bfloat16)
    return re, im


def stage_tables():
    re, im = dft_tables()

    def pair(a, b, c, d):
        return np.concatenate([np.concatenate([a, b], 1), np.concatenate([c, d], 1)], 0)

    first = [pair(re[:H, q::2], -im[:H, q::2], im[:H, q::2], re[:H, q::2]) for q in (0, 1)]
    second = pair(re, im, -im, re)
    third = [pair(re[q::2, :H], im[q::2, :H], -im[q::2, :H], re[q::2, :H]) for q in (0, 1)]
    fourth = pair(re, -im, im, re)
    return np.stack(first), second, np.stack(third), fourth


def slots_kernel(
    rule, places, first, last,
    rows_ref, cols_ref, count_ref, amp_ref, t1_ref, t2_ref, t3_ref, t4_ref, *refs,
):
    n_pieces = len(places)
    pieces = refs[:n_pieces]
    refs = refs[n_pieces:]
    if first:
        probe_ref = refs[0]
    refs = refs[1 if first else 4 :]
    ext, upd_ref, psum_ref, prb = refs[:4]
    pat, ext_b, exit_s, amp_buf = (refs[4 + 4 * i : 8 + 4 * i] for i in range(4))
    near_b, fold_b, back_b, lanes_buf, order, piece_sem, amp_sem = refs[20:]
    copies = []

    def bring(source, target):
        copies.append(pltpu.make_async_copy(source, target, piece_sem.at[len(copies)]))
        copies[-1].start()

    for piece, (r0, c0) in zip(pieces, places):
        _, h, w = piece.shape
        for b in range(w // H):
            bring(piece.at[:, :, b * H : (b + 1) * H], ext.at[:, c0 // H + b, r0 : r0 + h, :])

    def collect(s, n):
        order[n] = s
        keep = jnp.logical_and(s < count_ref[0, 0], rule(rows_ref[0, 0, s], cols_ref[0, 0, s]))
        return n + keep.astype(jnp.int32)

    total = lax.fori_loop(0, rows_ref.shape[2], collect, jnp.int32(0))

    def amp_copy(i, k=0):
        return pltpu.make_async_copy(amp_ref.at[0, 0, order[i]], amp_buf[k], amp_sem.at[k])

    if first:
        for b in range(2):
            bring(probe_ref.at[:, :, b * H : (b + 1) * H], lanes_buf.at[:, b])
        upd_ref[...] = jnp.zeros_like(upd_ref)
        psum_ref[...] = jnp.zeros_like(psum_ref)
    for copy in copies:
        copy.wait()
    if first:
        for comp in range(2):
            for q in range(2):
                for b in range(2):
                    prb[comp, q * H : (q + 1) * H, b * H : (b + 1) * H] = lanes_buf[comp, b, pl.ds(q, H, stride=2), :]

    lane = lax.broadcasted_iota(jnp.int32, (H, H), 1)

    dot = functools.partial(jnp.dot, preferred_element_type=jnp.float32)

    def place(i):
        s = order[i]
        c = cols_ref[0, 0, s]
        return rows_ref[0, 0, s], c // H, lax.rem(c, H)

    def enter(i, k, q):
        r, c0, off = place(i)
        back_shift = lax.rem(H - off, H)
        keep = lane < H - off
        part = []
        for comp in range(2):
            blocks = [pltpu.roll(ext[comp, c0 + b, pl.ds(r + q, H, stride=2), :], back_shift, 1) for b in range(3)]
            part.append([jnp.where(keep, blocks[b], blocks[b + 1]) for b in range(2)])
        for b in range(2):
            here = (slice(q * H, (q + 1) * H), slice(b * H, (b + 1) * H))
            pre, pim = prb[(0,) + here], prb[(1,) + here]
            are, aim = part[0][b], part[1][b]
            ere = pre * are - pim * aim
            eim = pre * aim + pim * are
            pat[k][(0,) + here] = are
            pat[k][(1,) + here] = aim
            exit_s[k][(0,) + here] = ere
            exit_s[k][(1,) + here] = eim
            ext_b[k][q, 0:H, b * H : (b + 1) * H] = ere.astype(jnp.bfloat16)
            ext_b[k][q, H:N, b * H : (b + 1) * H] = eim.astype(jnp.bfloat16)

    def near(k, m):
        even = dot(t1_ref[0], ext_b[k][0])
        odd = dot(t1_ref[1], ext_b[k][1])
        for comp in range(2):
            e, o = even[comp * H : (comp + 1) * H], odd[comp * H : (comp + 1) * H]
            near_b[m, 0:H, comp * N : (comp + 1) * N] = (e + o).astype(jnp.bfloat16)
            near_b[m, H:N, comp * N : (comp + 1) * N] = (e - o).astype(jnp.bfloat16)

    def project(k, m):
        far = dot(near_b[m], t2_ref[...])
        fre, fim = far[:, :N], far[:, N:]
        ratio = amp_buf[k][...].astype(jnp.float32) * lax.rsqrt(fre * fre + fim * fim + 0.25)
        for comp, part in enumerate((fre * ratio, fim * ratio)):
            top, low = part[:H], part[H:]
            fold_b[m, 0, comp * H : (comp + 1) * H, :] = (top + low).astype(jnp.bfloat16)
            fold_b[m, 1, comp * H : (comp + 1) * H, :] = (top - low).astype(jnp.bfloat16)

    def back(k, m, q):
        part = dot(t3_ref[q], fold_b[m, q])
        for comp in range(2):
            back_b[m, q * H : (q + 1) * H, comp * N : (comp + 1) * N] = part[comp * H : (comp + 1) * H].astype(
                jnp.bfloat16
            )

    def finish(i, k, m, q, live):
        r, c0, off = place(i)
        here = slice(q * H, (q + 1) * H)
        new = dot(back_b[m, here], t4_ref[...])
        dre = new[:, :N] - exit_s[k][0, here]
        dim = new[:, N:] - exit_s[k][1, here]
        if live is not None:
            dre, dim = dre * live, dim * live
        psum_ref[0, here] += pat[k][0, here] * dre + pat[k][1, here] * dim
        psum_ref[1, here] += pat[k][0, here] * dim - pat[k][1, here] * dre
        pre, pim = prb[0, here], prb[1, here]
        terms = (pre * dre + pim * dim, pre * dim - pim * dre)
        for comp in range(2):
            z0 = pltpu.roll(terms[comp][:, :H], off, 1)
            z1 = pltpu.roll(terms[comp][:, H:], off, 1)
            zero = jnp.zeros_like(z0)
            keep = lane >= off
            for b, val in enumerate((jnp.where(keep, z0, zero), jnp.where(keep, z1, z0), jnp.where(keep, zero, z1))):
                spot = (comp, c0 + b, pl.ds(r + q, H, stride=2), slice(None))
                upd_ref[spot] = upd_ref[spot] + val

    final = jnp.maximum(total - 1, 0)
    pairs = (total + 1) // 2

    def fetch(pair, half):
        for m in range(2):
            amp_copy(jnp.minimum(2 * pair + m, final), 2 * half + m).start()

    def work(pair, half):
        follow = jnp.minimum(pair + 1, pairs - 1)
        ids = [jnp.minimum(2 * pair + m, final) for m in range(2)]
        nxt = [jnp.minimum(2 * follow + m, final) for m in range(2)]
        live = (2 * pair + 1 < total).astype(jnp.float32)
        for m in range(2):
            amp_copy(ids[m], 2 * half + m).wait()
        for m in range(2):
            near(2 * half + m, m)
        enter(nxt[0], 2 * (1 - half), 0)
        for m in range(2):
            project(2 * half + m, m)
        enter(nxt[0], 2 * (1 - half), 1)
        for m in range(2):
            for q in range(2):
                back(2 * half + m, m, q)
        enter(nxt[1], 2 * (1 - half) + 1, 0)
        for m in range(2):
            for q in range(2):
                finish(ids[m], 2 * half + m, m, q, live if m else None)
        enter(nxt[1], 2 * (1 - half) + 1, 1)

    @pl.when(total > 0)
    def _():
        fetch(0, 0)
        for m in range(2):
            for q in range(2):
                enter(jnp.minimum(m, final), m, q)

    def step(j, carry):
        for half in range(2):
            pair = 2 * j + half

            def run(pair=pair, half=half):
                @pl.when(pair + 1 < pairs)
                def _():
                    fetch(pair + 1, 1 - half)

                work(pair, half)

            if half == 0:
                run()
            else:
                pl.when(pair < pairs)(run)
        return carry

    lax.fori_loop(0, (pairs + 1) // 2, step, 0)
    if last:
        for comp in range(2):
            for b in range(2):
                lanes = slice(b * H, (b + 1) * H)
                for q in range(2):
                    lanes_buf[comp, b, pl.ds(q, H, stride=2), :] = psum_ref[comp, q * H : (q + 1) * H, lanes]
                psum_ref[comp, :, lanes] = lanes_buf[comp, b]


def run_slots(rule, places, pieces, state, last, scalars, amplitudes, tables):
    smem = pl.BlockSpec(memory_space=pltpu.SMEM)
    vmem = pl.BlockSpec(memory_space=pltpu.VMEM)
    hbm = pl.BlockSpec(memory_space=pl.ANY)
    far = pl.BlockSpec(memory_space=pltpu.HBM)
    first = len(state) == 1
    shapes = [(2, WIDE // H, WIDE, H)] * 2 + [(2, N, N)] * 2
    at = 8 + len(pieces)
    return pl.pallas_call(
        functools.partial(slots_kernel, rule, places, first, last),
        out_shape=tuple(jax.ShapeDtypeStruct(shape, jnp.float32) for shape in shapes),
        in_specs=[smem] * 3 + [far] + [vmem] * 4 + [hbm] * len(pieces) + ([hbm] if first else [vmem] * 4),
        out_specs=(vmem,) * 4,
        input_output_aliases={} if first else {at + i: i for i in range(4)},
        scratch_shapes=[
            *[pltpu.VMEM((2, N, N), jnp.float32)] * 4,
            *[pltpu.VMEM((2, N, N), jnp.bfloat16)] * 4,
            *[pltpu.VMEM((2, N, N), jnp.float32)] * 4,
            *[pltpu.VMEM((N, N), jnp.bfloat16)] * 4,
            pltpu.VMEM((2, N, 2 * N), jnp.bfloat16),
            pltpu.VMEM((2, 2, N, N), jnp.bfloat16),
            pltpu.VMEM((2, N, 2 * N), jnp.bfloat16),
            pltpu.VMEM((2, 2, N, H), jnp.float32),
            pltpu.SMEM((40,), jnp.int32),
            pltpu.SemaphoreType.DMA((2 + sum(p.shape[2] // H for p in pieces),)),
            pltpu.SemaphoreType.DMA((4,)),
        ],
        compiler_params=pltpu.CompilerParams(vmem_limit_bytes=LIMIT),
        cost_estimate=pl.CostEstimate(flops=10_000_000_000, bytes_accessed=4_000_000, transcendentals=0),
    )(*scalars, amplitudes, *tables, *pieces, *state)


def passed_along(block, axis, distance):
    devices = range(lax.axis_size(axis))
    route = [(i - distance, i) for i in devices if i - distance in devices]
    return lax.ppermute(block, axis, route)


def from_diagonal(block):
    wide, tall = lax.axis_size("pos"), lax.axis_size("tile")
    route = [((p + 1) * tall + t + 1, p * tall + t) for p in range(wide - 1) for t in range(tall - 1)]
    return lax.ppermute(block, ("pos", "tile"), route)


def exchange_kernel(
    upd_ref, obj_ref, sum_ref, probe_ref, out_ref, grad_ref,
    from_left, from_above, corner, pair_in, part, x_in, piece, tile_in, gathered,
    right_send, right_recv, low_send, low_recv, pair_send, pair_recv, x_send, x_recv,
    t_send, t_recv, tg_send, tg_recv, xg_send, xg_recv, cg_send, cg_recv,
):
    p = lax.axis_index("pos")
    t = lax.axis_index("tile")
    x, z, core = p // 8, (p // 2) % 4, p % 2
    g = z * 4 + t

    def pos_of(xx, zz, cc):
        return xx * 8 + zz * 2 + cc

    right = {"pos": (p + 1) % 32, "tile": t}
    left = {"pos": (p + 31) % 32, "tile": t}
    below = {"pos": p, "tile": (t + 1) % 4}
    partner = {"pos": pos_of(x, z, 1 - core), "tile": t}
    x_peers = [{"pos": pos_of((x + d) % 4, z, core), "tile": t} for d in (1, 2, 3)]
    g_peers = [{"pos": pos_of(x, ((g + d) % 16) // 4, core), "tile": (g + d) % 4} for d in range(1, 16)]

    barrier = pltpu.get_barrier_semaphore()
    for peer in [right, left, partner] + x_peers + g_peers:
        pl.semaphore_signal(barrier, inc=1, device_id=peer, device_id_type=pl.DeviceIdType.MESH)
    pl.semaphore_wait(barrier, 21)

    started = []

    def send(source, target, send_sem, recv_sem, peer):
        copy = pltpu.make_async_remote_copy(
            src_ref=source, dst_ref=target, send_sem=send_sem, recv_sem=recv_sem,
            device_id=peer, device_id_type=pl.DeviceIdType.MESH,
        )
        copy.start()
        started.append(copy)
        return copy

    low1 = send(upd_ref.at[:, 2:4, 2 * N :, :], from_above.at[:, 2:4], low_send.at[0], low_recv.at[0], below)
    half = send(sum_ref.at[pl.ds((1 - core) * N, N)], pair_in, pair_send.at[0], pair_recv.at[0], partner)
    half.wait_recv()
    part[...] = sum_ref[pl.ds(core * N, N), :] + pair_in[...]
    x_copies = [
        send(part.at[pl.ds(((x + d) % 4) * 64, 64)], x_in.at[d - 1], x_send.at[d - 1], x_recv.at[d - 1], x_peers[d - 1])
        for d in (1, 2, 3)
    ]
    edge = send(upd_ref.at[:, 4:6, 2 * N :, :], from_left.at[:, :, 2 * N :, :], right_send.at[0], right_recv.at[0], right)
    has_left = (p > 0).astype(jnp.float32)
    has_above = (t > 0).astype(jnp.float32)
    power = jnp.sum(probe_ref[...] * probe_ref[...]) * (1.0 / (N * N)) + 1e-06
    scale = 1.0 / jnp.full((1, H), power, jnp.float32)

    for copy in x_copies:
        copy.wait_recv()
    shard = part[pl.ds(x * 64, 64), :] + x_in[0] + x_in[1] + x_in[2]
    for rg in range(8):
        for lg in range(2):
            piece[rg * 2 + lg] = shard[rg * 8 : rg * 8 + 8, lg * H : (lg + 1) * H]
    t_copies = [
        send(piece.at[(g + d) % 16], tile_in.at[d - 1], t_send.at[d - 1], t_recv.at[d - 1], g_peers[d - 1])
        for d in range(1, 16)
    ]
    mid = send(upd_ref.at[:, 4:6, N : 2 * N, :], from_left.at[:, :, N : 2 * N, :], right_send.at[1], right_recv.at[1], right)
    edge.wait_recv()
    corner[...] = upd_ref[:, 0:2, 2 * N :, :] + from_left[:, :, 2 * N :, :] * has_left

    for copy in t_copies:
        copy.wait_recv()
    own = piece[g]
    for d in range(15):
        own = own + tile_in[d]
    slots = 128 * 32
    gathered[core, x, g] = own * np.float32(1.0 / math.sqrt(slots))
    tg_copies = [
        send(gathered.at[core, x, g], gathered.at[core, x, g], tg_send.at[d - 1], tg_recv.at[d - 1], g_peers[d - 1])
        for d in range(1, 16)
    ]
    low0a = send(corner.at[:, 0], from_above.at[:, 0], low_send.at[1], low_recv.at[1], below)
    low0b = send(corner.at[:, 1], from_above.at[:, 1], low_send.at[2], low_recv.at[2], below)
    top = send(upd_ref.at[:, 4:6, :N, :], from_left.at[:, :, :N, :], right_send.at[2], right_recv.at[2], right)

    for copy in tg_copies:
        copy.wait_recv()
    xg_copies = [
        send(gathered.at[core, x], gathered.at[core, x], xg_send.at[d - 1], xg_recv.at[d - 1], x_peers[d - 1])
        for d in (1, 2, 3)
    ]
    cg_copies = [send(gathered.at[core, x], gathered.at[core, x], cg_send.at[0], cg_recv.at[0], partner)]

    def put(b, r0, value):
        for comp in range(2):
            here = (comp, slice(r0, r0 + N), slice(b * H, (b + 1) * H))
            out_ref[here] = obj_ref[here] + value[comp] * scale

    for b in (2, 3):
        put(b, N, upd_ref[:, b, N : 2 * N, :])
    for d in (1, 2, 3):
        xg_copies[d - 1].wait_recv()
        came = (x + 4 - d) % 4
        cg_copies.append(
            send(gathered.at[core, came], gathered.at[core, came], cg_send.at[d], cg_recv.at[d], partner)
        )
    mid.wait_recv()
    for b in (0, 1):
        put(b, N, upd_ref[:, b, N : 2 * N, :] + from_left[:, b, N : 2 * N, :] * has_left)
    low1.wait_recv()
    for b in (2, 3):
        put(b, 0, upd_ref[:, b, :N, :] + from_above[:, b] * has_above)
    top.wait_recv()
    for copy in cg_copies:
        copy.wait_recv()
    for h in range(2):
        for xx in range(4):
            for rg in range(8):
                for lg in range(2):
                    grad_ref[h, xx * 64 + rg * 8 : xx * 64 + rg * 8 + 8, lg * H : (lg + 1) * H] = gathered[h, xx, rg * 2 + lg]
    low0a.wait_recv()
    low0b.wait_recv()
    for b in (0, 1):
        put(b, 0, upd_ref[:, b, :N, :] + from_left[:, b, :N, :] * has_left + from_above[:, b] * has_above)
    for copy in started:
        copy.wait_send()


def exchange(update, object_field, total, probe):
    vmem = pl.BlockSpec(memory_space=pltpu.VMEM)
    f32 = jnp.float32
    dma = pltpu.SemaphoreType.DMA
    return pl.pallas_call(
        exchange_kernel,
        out_shape=(
            jax.ShapeDtypeStruct((2, BLOCK, BLOCK), f32),
            jax.ShapeDtypeStruct((2, N, N), f32),
        ),
        in_specs=[vmem] * 4,
        out_specs=(vmem, vmem),
        scratch_shapes=[
            pltpu.VMEM((2, 2, WIDE, H), f32),
            pltpu.VMEM((2, 4, N, H), f32),
            pltpu.VMEM((2, 2, N, H), f32),
            pltpu.VMEM((N, N), f32),
            pltpu.VMEM((N, N), f32),
            pltpu.VMEM((3, 64, N), f32),
            pltpu.VMEM((16, 8, H), f32),
            pltpu.VMEM((15, 8, H), f32),
            pltpu.VMEM((2, 4, 16, 8, H), f32),
            dma((3,)), dma((3,)), dma((3,)), dma((3,)), dma((1,)), dma((1,)), dma((3,)), dma((3,)),
            dma((15,)), dma((15,)), dma((15,)), dma((15,)), dma((3,)), dma((3,)), dma((4,)), dma((4,)),
        ],
        compiler_params=pltpu.CompilerParams(
            collective_id=0, has_side_effects=True, vmem_limit_bytes=32 * 1024 * 1024
        ),
    )(update, object_field, total, probe)


def shards(object_field, probe, amplitudes, corner_rows, corner_cols, counts):
    tables = [jnp.asarray(t) for t in stage_tables()]
    lows, corners = [], []
    for q in range(2):
        rows = slice(q * H, (q + 1) * H)
        lows.append(passed_along(object_field[:, rows, :], "tile", -1))
        corners.append(from_diagonal(object_field[:, rows, :N]))
    right = passed_along(object_field[:, :, :N], "pos", -1)
    fixed = ((corner_rows, corner_cols, counts), amplitudes, tables)
    reach = BLOCK - N
    state = run_slots(
        lambda r, c: (r <= reach) & (c <= reach), ((0, 0),), (object_field,), (probe,), False, *fixed
    )
    state = run_slots(lambda r, c: (r <= reach) & (c > reach), ((0, BLOCK),), (right,), state, False, *fixed)
    for q, rule in enumerate((lambda r, c: (r > reach) & (r <= reach + H), lambda r, c: r > reach + H)):
        row = BLOCK + q * H
        state = run_slots(rule, ((row, 0), (row, BLOCK)), (lows[q], corners[q]), state, q == 1, *fixed)
    _, update, total, _ = state
    return exchange(update, object_field, total.reshape(2 * N, N), probe)


def solution(mesh):
    return jax.shard_map(
        shards,
        mesh=mesh,
        in_specs=(
            P(None, "tile", "pos"),
            P(),
            P("tile", "pos", None, None, None),
            P("tile", "pos", None),
            P("tile", "pos", None),
            P("tile", "pos"),
        ),
        out_specs=(P(None, "tile", "pos"), P()),
        check_vma=False,
    )
```

```python
import functools
import math

import jax
import jax.numpy as jnp
import ml_dtypes
import numpy as np
from jax import lax
from jax.experimental import pallas as pl
from jax.experimental.pallas import tpu as pltpu
from jax.sharding import PartitionSpec as P

N = 256
H = 128
BLOCK = 512
WIDE = 768
LIMIT = 24 * 1024 * 1024


def dft_tables():
    j = np.arange(N)
    angle = (j[:, None] * j[None, :] % N) * (2.0 * np.pi / N)
    re = (np.cos(angle) / np.sqrt(N)).astype(np.float32).astype(ml_dtypes.bfloat16)
    im = (-np.sin(angle) / np.sqrt(N)).astype(np.float32).astype(ml_dtypes.bfloat16)
    return re, im


def stage_tables():
    re, im = dft_tables()

    def pair(a, b, c, d):
        return np.concatenate([np.concatenate([a, b], 1), np.concatenate([c, d], 1)], 0)

    first = [pair(re[:H, q::2], -im[:H, q::2], im[:H, q::2], re[:H, q::2]) for q in (0, 1)]
    second = pair(re, im, -im, re)
    third = [pair(re[q::2, :H], im[q::2, :H], -im[q::2, :H], re[q::2, :H]) for q in (0, 1)]
    fourth = pair(re, -im, im, re)
    return np.stack(first), second, np.stack(third), fourth


def slots_kernel(
    rule, places, first, last,
    rows_ref, cols_ref, count_ref, amp_ref, t1_ref, t2_ref, t3_ref, t4_ref, *refs,
):
    n_pieces = len(places)
    pieces = refs[:n_pieces]
    refs = refs[n_pieces:]
    if first:
        probe_ref = refs[0]
    refs = refs[1 if first else 4 :]
    ext, upd_ref, psum_ref, prb = refs[:4]
    pat, ext_b, exit_s, amp_buf = (refs[4 + 4 * i : 8 + 4 * i] for i in range(4))
    near_b, fold_b, back_b, lanes_buf, order, piece_sem, amp_sem = refs[20:]
    copies = []

    def bring(source, target):
        copies.append(pltpu.make_async_copy(source, target, piece_sem.at[len(copies)]))
        copies[-1].start()

    for piece, (r0, c0) in zip(pieces, places):
        _, h, w = piece.shape
        for b in range(w // H):
            bring(piece.at[:, :, b * H : (b + 1) * H], ext.at[:, c0 // H + b, r0 : r0 + h, :])

    def collect(s, n):
        order[n] = s
        keep = jnp.logical_and(s < count_ref[0, 0], rule(rows_ref[0, 0, s], cols_ref[0, 0, s]))
        return n + keep.astype(jnp.int32)

    total = lax.fori_loop(0, rows_ref.shape[2], collect, jnp.int32(0))

    def amp_copy(i, k=0):
        return pltpu.make_async_copy(amp_ref.at[0, 0, order[i]], amp_buf[k], amp_sem.at[k])

    final = jnp.maximum(total - 1, 0)
    pairs = (total + 1) // 2

    def fetch(pair, half):
        for m in range(2):
            amp_copy(jnp.minimum(2 * pair + m, final), 2 * half + m).start()

    @pl.when(total > 0)
    def _():
        fetch(0, 0)

    if first:
        for b in range(2):
            bring(probe_ref.at[:, :, b * H : (b + 1) * H], lanes_buf.at[:, b])
        upd_ref[...] = jnp.zeros_like(upd_ref)
        psum_ref[...] = jnp.zeros_like(psum_ref)
    for copy in copies:
        copy.wait()
    if first:
        for comp in range(2):
            for q in range(2):
                for b in range(2):
                    prb[comp, q * H : (q + 1) * H, b * H : (b + 1) * H] = lanes_buf[comp, b, pl.ds(q, H, stride=2), :]

    lane = lax.broadcasted_iota(jnp.int32, (H, H), 1)

    dot = functools.partial(jnp.dot, preferred_element_type=jnp.float32)

    def place(i):
        s = order[i]
        c = cols_ref[0, 0, s]
        return rows_ref[0, 0, s], c // H, lax.rem(c, H)

    def enter(i, k, q):
        r, c0, off = place(i)
        back_shift = lax.rem(H - off, H)
        keep = lane < H - off
        part = []
        for comp in range(2):
            blocks = [pltpu.roll(ext[comp, c0 + b, pl.ds(r + q, H, stride=2), :], back_shift, 1) for b in range(3)]
            part.append([jnp.where(keep, blocks[b], blocks[b + 1]) for b in range(2)])
        for b in range(2):
            here = (slice(q * H, (q + 1) * H), slice(b * H, (b + 1) * H))
            pre, pim = prb[(0,) + here], prb[(1,) + here]
            are, aim = part[0][b], part[1][b]
            ere = pre * are - pim * aim
            eim = pre * aim + pim * are
            pat[k][(0,) + here] = are
            pat[k][(1,) + here] = aim
            exit_s[k][(0,) + here] = ere
            exit_s[k][(1,) + here] = eim
            ext_b[k][q, 0:H, b * H : (b + 1) * H] = ere.astype(jnp.bfloat16)
            ext_b[k][q, H:N, b * H : (b + 1) * H] = eim.astype(jnp.bfloat16)

    def near(k, m):
        even = dot(t1_ref[0], ext_b[k][0])
        odd = dot(t1_ref[1], ext_b[k][1])
        for comp in range(2):
            e, o = even[comp * H : (comp + 1) * H], odd[comp * H : (comp + 1) * H]
            near_b[m, 0:H, comp * N : (comp + 1) * N] = (e + o).astype(jnp.bfloat16)
            near_b[m, H:N, comp * N : (comp + 1) * N] = (e - o).astype(jnp.bfloat16)

    def project(k, m):
        far = dot(near_b[m], t2_ref[...])
        fre, fim = far[:, :N], far[:, N:]
        ratio = amp_buf[k][...].astype(jnp.float32) * lax.rsqrt(fre * fre + fim * fim + 0.25)
        for comp, part in enumerate((fre * ratio, fim * ratio)):
            top, low = part[:H], part[H:]
            fold_b[m, 0, comp * H : (comp + 1) * H, :] = (top + low).astype(jnp.bfloat16)
            fold_b[m, 1, comp * H : (comp + 1) * H, :] = (top - low).astype(jnp.bfloat16)

    def back(k, m, q):
        part = dot(t3_ref[q], fold_b[m, q])
        for comp in range(2):
            back_b[m, q * H : (q + 1) * H, comp * N : (comp + 1) * N] = part[comp * H : (comp + 1) * H].astype(
                jnp.bfloat16
            )

    def finish(i, k, m, q, live):
        r, c0, off = place(i)
        here = slice(q * H, (q + 1) * H)
        new = dot(back_b[m, here], t4_ref[...])
        dre = new[:, :N] - exit_s[k][0, here]
        dim = new[:, N:] - exit_s[k][1, here]
        if live is not None:
            dre, dim = dre * live, dim * live
        psum_ref[0, here] += pat[k][0, here] * dre + pat[k][1, here] * dim
        psum_ref[1, here] += pat[k][0, here] * dim - pat[k][1, here] * dre
        pre, pim = prb[0, here], prb[1, here]
        terms = (pre * dre + pim * dim, pre * dim - pim * dre)
        for comp in range(2):
            z0 = pltpu.roll(terms[comp][:, :H], off, 1)
            z1 = pltpu.roll(terms[comp][:, H:], off, 1)
            zero = jnp.zeros_like(z0)
            keep = lane >= off
            for b, val in enumerate((jnp.where(keep, z0, zero), jnp.where(keep, z1, z0), jnp.where(keep, zero, z1))):
                spot = (comp, c0 + b, pl.ds(r + q, H, stride=2), slice(None))
                upd_ref[spot] = upd_ref[spot] + val

    def work(pair, half):
        follow = jnp.minimum(pair + 1, pairs - 1)
        ids = [jnp.minimum(2 * pair + m, final) for m in range(2)]
        nxt = [jnp.minimum(2 * follow + m, final) for m in range(2)]
        live = (2 * pair + 1 < total).astype(jnp.float32)
        for m in range(2):
            amp_copy(ids[m], 2 * half + m).wait()
        for m in range(2):
            near(2 * half + m, m)
        enter(nxt[0], 2 * (1 - half), 0)
        for m in range(2):
            project(2 * half + m, m)
        enter(nxt[0], 2 * (1 - half), 1)
        for m in range(2):
            for q in range(2):
                back(2 * half + m, m, q)
        enter(nxt[1], 2 * (1 - half) + 1, 0)
        for m in range(2):
            for q in range(2):
                finish(ids[m], 2 * half + m, m, q, live if m else None)
        enter(nxt[1], 2 * (1 - half) + 1, 1)

    @pl.when(total > 0)
    def _():
        for m in range(2):
            for q in range(2):
                enter(jnp.minimum(m, final), m, q)

    def step(j, carry):
        for half in range(2):
            pair = 2 * j + half

            def run(pair=pair, half=half):
                @pl.when(pair + 1 < pairs)
                def _():
                    fetch(pair + 1, 1 - half)

                work(pair, half)

            if half == 0:
                run()
            else:
                pl.when(pair < pairs)(run)
        return carry

    lax.fori_loop(0, (pairs + 1) // 2, step, 0)
    if last:
        for comp in range(2):
            for b in range(2):
                lanes = slice(b * H, (b + 1) * H)
                for q in range(2):
                    lanes_buf[comp, b, pl.ds(q, H, stride=2), :] = psum_ref[comp, q * H : (q + 1) * H, lanes]
                psum_ref[comp, :, lanes] = lanes_buf[comp, b]


def run_slots(rule, places, pieces, state, last, scalars, amplitudes, tables):
    smem = pl.BlockSpec(memory_space=pltpu.SMEM)
    vmem = pl.BlockSpec(memory_space=pltpu.VMEM)
    hbm = pl.BlockSpec(memory_space=pl.ANY)
    far = pl.BlockSpec(memory_space=pltpu.HBM)
    first = len(state) == 1
    shapes = [(2, WIDE // H, WIDE, H)] * 2 + [(2, N, N)] * 2
    at = 8 + len(pieces)
    return pl.pallas_call(
        functools.partial(slots_kernel, rule, places, first, last),
        out_shape=tuple(jax.ShapeDtypeStruct(shape, jnp.float32) for shape in shapes),
        in_specs=[smem] * 3 + [far] + [vmem] * 4 + [hbm] * len(pieces) + ([hbm] if first else [vmem] * 4),
        out_specs=(vmem,) * 4,
        input_output_aliases={} if first else {at + i: i for i in range(4)},
        scratch_shapes=[
            *[pltpu.VMEM((2, N, N), jnp.float32)] * 4,
            *[pltpu.VMEM((2, N, N), jnp.bfloat16)] * 4,
            *[pltpu.VMEM((2, N, N), jnp.float32)] * 4,
            *[pltpu.VMEM((N, N), jnp.bfloat16)] * 4,
            pltpu.VMEM((2, N, 2 * N), jnp.bfloat16),
            pltpu.VMEM((2, 2, N, N), jnp.bfloat16),
            pltpu.VMEM((2, N, 2 * N), jnp.bfloat16),
            pltpu.VMEM((2, 2, N, H), jnp.float32),
            pltpu.SMEM((40,), jnp.int32),
            pltpu.SemaphoreType.DMA((2 + sum(p.shape[2] // H for p in pieces),)),
            pltpu.SemaphoreType.DMA((4,)),
        ],
        compiler_params=pltpu.CompilerParams(vmem_limit_bytes=LIMIT),
        cost_estimate=pl.CostEstimate(flops=10_000_000_000, bytes_accessed=4_000_000, transcendentals=0),
    )(*scalars, amplitudes, *tables, *pieces, *state)


def passed_along(block, axis, distance):
    devices = range(lax.axis_size(axis))
    route = [(i - distance, i) for i in devices if i - distance in devices]
    return lax.ppermute(block, axis, route)


def from_diagonal(block):
    wide, tall = lax.axis_size("pos"), lax.axis_size("tile")
    route = [((p + 1) * tall + t + 1, p * tall + t) for p in range(wide - 1) for t in range(tall - 1)]
    return lax.ppermute(block, ("pos", "tile"), route)


def exchange_kernel(
    upd_ref, obj_ref, sum_ref, probe_ref, out_ref, grad_ref,
    from_left, from_above, corner, pair_in, part, x_in, piece, z_in, y_in, gathered,
    right_send, right_recv, low_send, low_recv, pair_send, pair_recv, x_send, x_recv,
    z_send, z_recv, y_send, y_recv, zg_send, zg_recv, xg_send, xg_recv, cg_send, cg_recv,
):
    p = lax.axis_index("pos")
    t = lax.axis_index("tile")
    x, z, core = p // 8, (p // 2) % 4, p % 2

    def pos_of(xx, zz, cc):
        return xx * 8 + zz * 2 + cc

    right = {"pos": (p + 1) % 32, "tile": t}
    left = {"pos": (p + 31) % 32, "tile": t}
    below = {"pos": p, "tile": (t + 1) % 4}
    partner = {"pos": pos_of(x, z, 1 - core), "tile": t}
    x_peers = [{"pos": pos_of((x + d) % 4, z, core), "tile": t} for d in (1, 2, 3)]
    z_peers = [{"pos": pos_of(x, (z + d) % 4, core), "tile": t} for d in (1, 2, 3)]
    y_peers = [{"pos": p, "tile": (t + d) % 4} for d in (1, 2, 3)]

    barrier = pltpu.get_barrier_semaphore()
    peers = [right, left, partner] + x_peers + z_peers + y_peers
    for peer in peers:
        pl.semaphore_signal(barrier, inc=1, device_id=peer, device_id_type=pl.DeviceIdType.MESH)
    pl.semaphore_wait(barrier, len(peers))

    started = []

    def send(source, target, send_sem, recv_sem, peer):
        copy = pltpu.make_async_remote_copy(
            src_ref=source, dst_ref=target, send_sem=send_sem, recv_sem=recv_sem,
            device_id=peer, device_id_type=pl.DeviceIdType.MESH,
        )
        copy.start()
        started.append(copy)
        return copy

    edge = send(upd_ref.at[:, 4:6, 2 * N :, :], from_left.at[:, :, 2 * N :, :], right_send.at[0], right_recv.at[0], right)
    low1 = send(upd_ref.at[:, 2, 2 * N :, :], from_above.at[:, 2], low_send.at[0], low_recv.at[0], below)
    half = send(sum_ref.at[pl.ds((1 - core) * N, N)], pair_in, pair_send.at[0], pair_recv.at[0], partner)
    half.wait_recv()
    part[...] = sum_ref[pl.ds(core * N, N), :] + pair_in[...]
    x_copies = [
        send(part.at[pl.ds(((x + d) % 4) * 64, 64)], x_in.at[d - 1], x_send.at[d - 1], x_recv.at[d - 1], x_peers[d - 1])
        for d in (1, 2, 3)
    ]
    has_left = (p > 0).astype(jnp.float32)
    has_above = (t > 0).astype(jnp.float32)
    power = jnp.sum(probe_ref[...] * probe_ref[...]) * (1.0 / (N * N)) + 1e-06
    scale = 1.0 / jnp.full((1, H), power, jnp.float32)

    for copy in x_copies:
        copy.wait_recv()
    shard = part[pl.ds(x * 64, 64), :] + x_in[0] + x_in[1] + x_in[2]
    for rg in range(8):
        for lg in range(2):
            piece[rg * 2 + lg] = shard[rg * 8 : rg * 8 + 8, lg * H : (lg + 1) * H]
    z_copies = [
        send(piece.at[pl.ds(((z + d) % 4) * 4, 4)], z_in.at[d - 1], z_send.at[d - 1], z_recv.at[d - 1], z_peers[d - 1])
        for d in (1, 2, 3)
    ]
    low2 = send(upd_ref.at[:, 3, 2 * N :, :], from_above.at[:, 3], low_send.at[3], low_recv.at[3], below)
    mid = send(upd_ref.at[:, 4:6, N : 2 * N, :], from_left.at[:, :, N : 2 * N, :], right_send.at[1], right_recv.at[1], right)
    for copy in z_copies:
        copy.wait_recv()
    y_in[t] = piece[pl.ds(z * 4, 4)] + z_in[0] + z_in[1] + z_in[2]
    y_copies = [send(y_in.at[t], y_in.at[t], y_send.at[d - 1], y_recv.at[d - 1], y_peers[d - 1]) for d in (1, 2, 3)]
    edge.wait_recv()
    corner[...] = upd_ref[:, 0:2, 2 * N :, :] + from_left[:, :, 2 * N :, :] * has_left
    low0a = send(corner.at[:, 0], from_above.at[:, 0], low_send.at[1], low_recv.at[1], below)
    low0b = send(corner.at[:, 1], from_above.at[:, 1], low_send.at[2], low_recv.at[2], below)

    for copy in y_copies:
        copy.wait_recv()
    slots = 128 * 32
    mine = gathered.at[core, x, pl.ds(z * 4, 4)]
    mine[...] = (y_in[0] + y_in[1] + y_in[2] + y_in[3]) * np.float32(1.0 / math.sqrt(slots))
    zg_copies = [send(mine, mine, zg_send.at[d - 1], zg_recv.at[d - 1], z_peers[d - 1]) for d in (1, 2, 3)]
    top = send(upd_ref.at[:, 4:6, :N, :], from_left.at[:, :, :N, :], right_send.at[2], right_recv.at[2], right)

    for copy in zg_copies:
        copy.wait_recv()
    xg_copies = [
        send(gathered.at[core, x], gathered.at[core, x], xg_send.at[d - 1], xg_recv.at[d - 1], x_peers[d - 1])
        for d in (1, 2, 3)
    ]
    cg_copies = [send(gathered.at[core, x], gathered.at[core, x], cg_send.at[0], cg_recv.at[0], partner)]

    def put(b, r0, value):
        for comp in range(2):
            here = (comp, slice(r0, r0 + N), slice(b * H, (b + 1) * H))
            out_ref[here] = obj_ref[here] + value[comp] * scale

    for b in (2, 3):
        put(b, N, upd_ref[:, b, N : 2 * N, :])
    for d in (1, 2, 3):
        xg_copies[d - 1].wait_recv()
        came = (x + 4 - d) % 4
        cg_copies.append(
            send(gathered.at[core, came], gathered.at[core, came], cg_send.at[d], cg_recv.at[d], partner)
        )
    mid.wait_recv()
    for b in (0, 1):
        put(b, N, upd_ref[:, b, N : 2 * N, :] + from_left[:, b, N : 2 * N, :] * has_left)
    low1.wait_recv()
    low2.wait_recv()
    for b in (2, 3):
        put(b, 0, upd_ref[:, b, :N, :] + from_above[:, b] * has_above)
    top.wait_recv()
    for copy in cg_copies:
        copy.wait_recv()
    for h in range(2):
        for xx in range(4):
            for rg in range(8):
                for lg in range(2):
                    grad_ref[h, xx * 64 + rg * 8 : xx * 64 + rg * 8 + 8, lg * H : (lg + 1) * H] = gathered[h, xx, rg * 2 + lg]
    low0a.wait_recv()
    low0b.wait_recv()
    for b in (0, 1):
        put(b, 0, upd_ref[:, b, :N, :] + from_left[:, b, :N, :] * has_left + from_above[:, b] * has_above)
    for copy in started:
        copy.wait_send()


def exchange(update, object_field, total, probe):
    vmem = pl.BlockSpec(memory_space=pltpu.VMEM)
    f32 = jnp.float32
    dma = pltpu.SemaphoreType.DMA
    return pl.pallas_call(
        exchange_kernel,
        out_shape=(
            jax.ShapeDtypeStruct((2, BLOCK, BLOCK), f32),
            jax.ShapeDtypeStruct((2, N, N), f32),
        ),
        in_specs=[vmem] * 4,
        out_specs=(vmem, vmem),
        scratch_shapes=[
            pltpu.VMEM((2, 2, WIDE, H), f32),
            pltpu.VMEM((2, 4, N, H), f32),
            pltpu.VMEM((2, 2, N, H), f32),
            pltpu.VMEM((N, N), f32),
            pltpu.VMEM((N, N), f32),
            pltpu.VMEM((3, 64, N), f32),
            pltpu.VMEM((16, 8, H), f32),
            pltpu.VMEM((3, 4, 8, H), f32),
            pltpu.VMEM((4, 4, 8, H), f32),
            pltpu.VMEM((2, 4, 16, 8, H), f32),
            dma((3,)), dma((3,)), dma((4,)), dma((4,)), dma((1,)), dma((1,)), dma((3,)), dma((3,)),
            *[dma((3,))] * 8, dma((4,)), dma((4,)),
        ],
        compiler_params=pltpu.CompilerParams(
            collective_id=0, has_side_effects=True, vmem_limit_bytes=32 * 1024 * 1024
        ),
    )(update, object_field, total, probe)


def shards(object_field, probe, amplitudes, corner_rows, corner_cols, counts):
    tables = [jnp.asarray(t) for t in stage_tables()]
    right = passed_along(object_field[:, :, :N], "pos", -1)
    low = passed_along(object_field[:, :N, :], "tile", -1)
    corner = from_diagonal(object_field[:, :N, :N])
    amplitudes = pltpu.with_memory_space_constraint(amplitudes, pltpu.HBM)
    fixed = ((corner_rows, corner_cols, counts), amplitudes, tables)
    reach = BLOCK - N
    state = run_slots(
        lambda r, c: (r <= reach) & (c <= reach), ((0, 0),), (object_field,), (probe,), False, *fixed
    )
    state = run_slots(lambda r, c: (r <= reach) & (c > reach), ((0, BLOCK),), (right,), state, False, *fixed)
    state = run_slots(lambda r, c: (r > reach) & (c <= reach), ((BLOCK, 0),), (low,), state, False, *fixed)
    _, update, total, _ = run_slots(
        lambda r, c: (r > reach) & (c > reach), ((BLOCK, BLOCK),), (corner,), state, True, *fixed
    )
    return exchange(update, object_field, total.reshape(2 * N, N), probe)


def solution(mesh):
    return jax.shard_map(
        shards,
        mesh=mesh,
        in_specs=(
            P(None, "tile", "pos"),
            P(),
            P("tile", "pos", None, None, None),
            P("tile", "pos", None),
            P("tile", "pos", None),
            P("tile", "pos"),
        ),
        out_specs=(P(None, "tile", "pos"), P()),
        check_vma=False,
    )
```

```python
import functools
import math

import jax
import jax.numpy as jnp
import ml_dtypes
import numpy as np
from jax import lax
from jax.experimental import pallas as pl
from jax.experimental.pallas import tpu as pltpu
from jax.sharding import PartitionSpec as P

N = 256
H = 128
BLOCK = 512
WIDE = 768
LIMIT = 24 * 1024 * 1024


def dft_tables():
    j = np.arange(N)
    angle = (j[:, None] * j[None, :] % N) * (2.0 * np.pi / N)
    re = (np.cos(angle) / np.sqrt(N)).astype(np.float32).astype(ml_dtypes.bfloat16)
    im = (-np.sin(angle) / np.sqrt(N)).astype(np.float32).astype(ml_dtypes.bfloat16)
    return re, im


def stage_tables():
    re, im = dft_tables()

    def pair(a, b, c, d):
        return np.concatenate([np.concatenate([a, b], 1), np.concatenate([c, d], 1)], 0)

    first = [pair(re[:H, q::2], -im[:H, q::2], im[:H, q::2], re[:H, q::2]) for q in (0, 1)]
    second = pair(re, im, -im, re)
    third = [pair(re[q::2, :H], im[q::2, :H], -im[q::2, :H], re[q::2, :H]) for q in (0, 1)]
    fourth = pair(re, -im, im, re)
    return np.stack(first), second, np.stack(third), fourth


def slots_kernel(
    rule, places, first, last,
    rows_ref, cols_ref, count_ref, amp_ref, t1_ref, t2_ref, t3_ref, t4_ref, *refs,
):
    n_pieces = len(places)
    pieces = refs[:n_pieces]
    refs = refs[n_pieces:]
    if first:
        probe_ref = refs[0]
    refs = refs[1 if first else 4 :]
    ext, upd_ref, psum_ref, prb = refs[:4]
    pat, ext_b, exit_s, amp_buf = (refs[4 + 4 * i : 8 + 4 * i] for i in range(4))
    near_b, fold_b, back_b, lanes_buf, order, piece_sem, amp_sem = refs[20:]
    copies = []

    def bring(source, target):
        copies.append(pltpu.make_async_copy(source, target, piece_sem.at[len(copies)]))
        copies[-1].start()

    for piece, (r0, c0) in zip(pieces, places):
        _, h, w = piece.shape
        for b in range(w // H):
            bring(piece.at[:, :, b * H : (b + 1) * H], ext.at[:, c0 // H + b, r0 : r0 + h, :])

    def collect(s, n):
        order[n] = s
        keep = jnp.logical_and(s < count_ref[0, 0], rule(rows_ref[0, 0, s], cols_ref[0, 0, s]))
        return n + keep.astype(jnp.int32)

    total = lax.fori_loop(0, rows_ref.shape[2], collect, jnp.int32(0))

    def amp_copy(i, k=0):
        return pltpu.make_async_copy(amp_ref.at[0, 0, order[i]], amp_buf[k], amp_sem.at[k])

    final = jnp.maximum(total - 1, 0)
    pairs = (total + 1) // 2

    def fetch(pair, half):
        for m in range(2):
            amp_copy(jnp.minimum(2 * pair + m, final), 2 * half + m).start()

    @pl.when(total > 0)
    def _():
        fetch(0, 0)

    if first:
        for b in range(2):
            bring(probe_ref.at[:, :, b * H : (b + 1) * H], lanes_buf.at[:, b])
        upd_ref[...] = jnp.zeros_like(upd_ref)
        psum_ref[...] = jnp.zeros_like(psum_ref)
    for copy in copies:
        copy.wait()
    if first:
        for comp in range(2):
            for q in range(2):
                for b in range(2):
                    prb[comp, q * H : (q + 1) * H, b * H : (b + 1) * H] = lanes_buf[comp, b, pl.ds(q, H, stride=2), :]

    lane = lax.broadcasted_iota(jnp.int32, (H, H), 1)

    dot = functools.partial(jnp.dot, preferred_element_type=jnp.float32)

    def place(i):
        s = order[i]
        c = cols_ref[0, 0, s]
        return rows_ref[0, 0, s], c // H, lax.rem(c, H)

    def enter(i, k, q):
        r, c0, off = place(i)
        back_shift = lax.rem(H - off, H)
        keep = lane < H - off
        part = []
        for comp in range(2):
            blocks = [pltpu.roll(ext[comp, c0 + b, pl.ds(r + q, H, stride=2), :], back_shift, 1) for b in range(3)]
            part.append([jnp.where(keep, blocks[b], blocks[b + 1]) for b in range(2)])
        for b in range(2):
            here = (slice(q * H, (q + 1) * H), slice(b * H, (b + 1) * H))
            pre, pim = prb[(0,) + here], prb[(1,) + here]
            are, aim = part[0][b], part[1][b]
            ere = pre * are - pim * aim
            eim = pre * aim + pim * are
            pat[k][(0,) + here] = are
            pat[k][(1,) + here] = aim
            exit_s[k][(0,) + here] = ere
            exit_s[k][(1,) + here] = eim
            ext_b[k][q, 0:H, b * H : (b + 1) * H] = ere.astype(jnp.bfloat16)
            ext_b[k][q, H:N, b * H : (b + 1) * H] = eim.astype(jnp.bfloat16)

    def near(k, m):
        even = dot(t1_ref[0], ext_b[k][0])
        odd = dot(t1_ref[1], ext_b[k][1])
        for comp in range(2):
            e, o = even[comp * H : (comp + 1) * H], odd[comp * H : (comp + 1) * H]
            near_b[m, 0:H, comp * N : (comp + 1) * N] = (e + o).astype(jnp.bfloat16)
            near_b[m, H:N, comp * N : (comp + 1) * N] = (e - o).astype(jnp.bfloat16)

    def project(k, m):
        far = dot(near_b[m], t2_ref[...])
        fre, fim = far[:, :N], far[:, N:]
        ratio = amp_buf[k][...].astype(jnp.float32) * lax.rsqrt(fre * fre + fim * fim + 0.25)
        for comp, part in enumerate((fre * ratio, fim * ratio)):
            top, low = part[:H], part[H:]
            fold_b[m, 0, comp * H : (comp + 1) * H, :] = (top + low).astype(jnp.bfloat16)
            fold_b[m, 1, comp * H : (comp + 1) * H, :] = (top - low).astype(jnp.bfloat16)

    def back(k, m, q):
        part = dot(t3_ref[q], fold_b[m, q])
        for comp in range(2):
            back_b[m, q * H : (q + 1) * H, comp * N : (comp + 1) * N] = part[comp * H : (comp + 1) * H].astype(
                jnp.bfloat16
            )

    def finish(i, k, m, q, live):
        r, c0, off = place(i)
        here = slice(q * H, (q + 1) * H)
        new = dot(back_b[m, here], t4_ref[...])
        dre = new[:, :N] - exit_s[k][0, here]
        dim = new[:, N:] - exit_s[k][1, here]
        if live is not None:
            dre, dim = dre * live, dim * live
        psum_ref[0, here] += pat[k][0, here] * dre + pat[k][1, here] * dim
        psum_ref[1, here] += pat[k][0, here] * dim - pat[k][1, here] * dre
        pre, pim = prb[0, here], prb[1, here]
        terms = (pre * dre + pim * dim, pre * dim - pim * dre)
        for comp in range(2):
            z0 = pltpu.roll(terms[comp][:, :H], off, 1)
            z1 = pltpu.roll(terms[comp][:, H:], off, 1)
            zero = jnp.zeros_like(z0)
            keep = lane >= off
            for b, val in enumerate((jnp.where(keep, z0, zero), jnp.where(keep, z1, z0), jnp.where(keep, zero, z1))):
                spot = (comp, c0 + b, pl.ds(r + q, H, stride=2), slice(None))
                upd_ref[spot] = upd_ref[spot] + val

    def work(pair, half):
        follow = jnp.minimum(pair + 1, pairs - 1)
        ids = [jnp.minimum(2 * pair + m, final) for m in range(2)]
        nxt = [jnp.minimum(2 * follow + m, final) for m in range(2)]
        live = (2 * pair + 1 < total).astype(jnp.float32)
        for m in range(2):
            amp_copy(ids[m], 2 * half + m).wait()
        for m in range(2):
            near(2 * half + m, m)
        enter(nxt[0], 2 * (1 - half), 0)
        for m in range(2):
            project(2 * half + m, m)
        enter(nxt[0], 2 * (1 - half), 1)
        for m in range(2):
            for q in range(2):
                back(2 * half + m, m, q)
        enter(nxt[1], 2 * (1 - half) + 1, 0)
        for m in range(2):
            for q in range(2):
                finish(ids[m], 2 * half + m, m, q, live if m else None)
        enter(nxt[1], 2 * (1 - half) + 1, 1)

    @pl.when(total > 0)
    def _():
        for m in range(2):
            for q in range(2):
                enter(jnp.minimum(m, final), m, q)

    def step(j, carry):
        for half in range(2):
            pair = 2 * j + half

            def run(pair=pair, half=half):
                @pl.when(pair + 1 < pairs)
                def _():
                    fetch(pair + 1, 1 - half)

                work(pair, half)

            if half == 0:
                run()
            else:
                pl.when(pair < pairs)(run)
        return carry

    lax.fori_loop(0, (pairs + 1) // 2, step, 0)
    if last:
        for comp in range(2):
            for b in range(2):
                lanes = slice(b * H, (b + 1) * H)
                for q in range(2):
                    lanes_buf[comp, b, pl.ds(q, H, stride=2), :] = psum_ref[comp, q * H : (q + 1) * H, lanes]
                psum_ref[comp, :, lanes] = lanes_buf[comp, b]


def run_slots(rule, places, pieces, state, last, scalars, amplitudes, tables):
    smem = pl.BlockSpec(memory_space=pltpu.SMEM)
    vmem = pl.BlockSpec(memory_space=pltpu.VMEM)
    hbm = pl.BlockSpec(memory_space=pl.ANY)
    far = pl.BlockSpec(memory_space=pltpu.HBM)
    first = len(state) == 1
    shapes = [(2, WIDE // H, WIDE, H)] * 2 + [(2, N, N)] * 2
    at = 8 + len(pieces)
    return pl.pallas_call(
        functools.partial(slots_kernel, rule, places, first, last),
        out_shape=tuple(jax.ShapeDtypeStruct(shape, jnp.float32) for shape in shapes),
        in_specs=[smem] * 3 + [far] + [vmem] * 4 + [hbm] * len(pieces) + ([hbm] if first else [vmem] * 4),
        out_specs=(vmem,) * 4,
        input_output_aliases={} if first else {at + i: i for i in range(4)},
        scratch_shapes=[
            *[pltpu.VMEM((2, N, N), jnp.float32)] * 4,
            *[pltpu.VMEM((2, N, N), jnp.bfloat16)] * 4,
            *[pltpu.VMEM((2, N, N), jnp.float32)] * 4,
            *[pltpu.VMEM((N, N), jnp.bfloat16)] * 4,
            pltpu.VMEM((2, N, 2 * N), jnp.bfloat16),
            pltpu.VMEM((2, 2, N, N), jnp.bfloat16),
            pltpu.VMEM((2, N, 2 * N), jnp.bfloat16),
            pltpu.VMEM((2, 2, N, H), jnp.float32),
            pltpu.SMEM((40,), jnp.int32),
            pltpu.SemaphoreType.DMA((2 + sum(p.shape[2] // H for p in pieces),)),
            pltpu.SemaphoreType.DMA((4,)),
        ],
        compiler_params=pltpu.CompilerParams(vmem_limit_bytes=LIMIT),
        cost_estimate=pl.CostEstimate(flops=10_000_000_000, bytes_accessed=4_000_000, transcendentals=0),
    )(*scalars, amplitudes, *tables, *pieces, *state)


def passed_along(block, axis, distance):
    devices = range(lax.axis_size(axis))
    route = [(i - distance, i) for i in devices if i - distance in devices]
    return lax.ppermute(block, axis, route)


def from_diagonal(block):
    wide, tall = lax.axis_size("pos"), lax.axis_size("tile")
    route = [((p + 1) * tall + t + 1, p * tall + t) for p in range(wide - 1) for t in range(tall - 1)]
    return lax.ppermute(block, ("pos", "tile"), route)


def exchange_kernel(
    upd_ref, obj_ref, sum_ref, probe_ref, out_ref, grad_ref,
    from_left, from_above, corner, pair_in, part, x_in, piece, z_in, y_in, gathered,
    right_send, right_recv, low_send, low_recv, pair_send, pair_recv, x_send, x_recv,
    z_send, z_recv, y_send, y_recv, zg_send, zg_recv, xg_send, xg_recv, cg_send, cg_recv,
):
    p = lax.axis_index("pos")
    t = lax.axis_index("tile")
    x, z, core = p // 8, (p // 2) % 4, p % 2

    def pos_of(xx, zz, cc):
        return xx * 8 + zz * 2 + cc

    right = {"pos": (p + 1) % 32, "tile": t}
    left = {"pos": (p + 31) % 32, "tile": t}
    below = {"pos": p, "tile": (t + 1) % 4}
    partner = {"pos": pos_of(x, z, 1 - core), "tile": t}
    x_peers = [{"pos": pos_of((x + d) % 4, z, core), "tile": t} for d in (1, 2, 3)]
    z_peers = [{"pos": pos_of(x, (z + d) % 4, core), "tile": t} for d in (1, 2, 3)]
    y_peers = [{"pos": p, "tile": (t + d) % 4} for d in (1, 2, 3)]

    barrier = pltpu.get_barrier_semaphore()
    peers = [right, left, partner] + x_peers + z_peers + y_peers
    for peer in peers:
        pl.semaphore_signal(barrier, inc=1, device_id=peer, device_id_type=pl.DeviceIdType.MESH)
    pl.semaphore_wait(barrier, len(peers))

    started, rims = [], []
    sends_right, sends_low, has_left, has_above = p < 31, t < 3, p > 0, t > 0

    def describe(source, target, send_sem, recv_sem, peer):
        return pltpu.make_async_remote_copy(
            src_ref=source, dst_ref=target, send_sem=send_sem, recv_sem=recv_sem,
            device_id=peer, device_id_type=pl.DeviceIdType.MESH,
        )

    def send(*where):
        copy = describe(*where)
        copy.start()
        started.append(copy)
        return copy

    def send_rim(go, *where):
        copy = describe(*where)
        pl.when(go)(copy.start)
        rims.append((go, copy))
        return copy

    @pl.when(p == 0)
    def _():
        from_left[...] = jnp.zeros_like(from_left)

    @pl.when(t == 0)
    def _():
        from_above[...] = jnp.zeros_like(from_above)

    edge = send_rim(sends_right, upd_ref.at[:, 4:6, 2 * N :, :], from_left.at[:, :, 2 * N :, :], right_send.at[0], right_recv.at[0], right)
    low1 = send_rim(sends_low, upd_ref.at[:, 2, 2 * N :, :], from_above.at[:, 2], low_send.at[0], low_recv.at[0], below)
    half = send(sum_ref.at[pl.ds((1 - core) * N, N)], pair_in, pair_send.at[0], pair_recv.at[0], partner)
    half.wait_recv()
    part[...] = sum_ref[pl.ds(core * N, N), :] + pair_in[...]
    x_copies = [
        send(part.at[pl.ds(((x + d) % 4) * 64, 64)], x_in.at[d - 1], x_send.at[d - 1], x_recv.at[d - 1], x_peers[d - 1])
        for d in (1, 2, 3)
    ]
    power = jnp.sum(probe_ref[...] * probe_ref[...]) * (1.0 / (N * N)) + 1e-06
    scale = 1.0 / jnp.full((1, H), power, jnp.float32)

    for copy in x_copies:
        copy.wait_recv()
    shard = part[pl.ds(x * 64, 64), :] + x_in[0] + x_in[1] + x_in[2]
    for rg in range(8):
        for lg in range(2):
            piece[rg * 2 + lg] = shard[rg * 8 : rg * 8 + 8, lg * H : (lg + 1) * H]
    z_copies = [
        send(piece.at[pl.ds(((z + d) % 4) * 4, 4)], z_in.at[d - 1], z_send.at[d - 1], z_recv.at[d - 1], z_peers[d - 1])
        for d in (1, 2, 3)
    ]
    low2 = send_rim(sends_low, upd_ref.at[:, 3, 2 * N :, :], from_above.at[:, 3], low_send.at[3], low_recv.at[3], below)
    mid = send_rim(sends_right, upd_ref.at[:, 4:6, N : 2 * N, :], from_left.at[:, :, N : 2 * N, :], right_send.at[1], right_recv.at[1], right)
    for copy in z_copies:
        copy.wait_recv()
    y_in[t] = piece[pl.ds(z * 4, 4)] + z_in[0] + z_in[1] + z_in[2]
    y_copies = [send(y_in.at[t], y_in.at[t], y_send.at[d - 1], y_recv.at[d - 1], y_peers[d - 1]) for d in (1, 2, 3)]
    pl.when(has_left)(edge.wait_recv)
    corner[...] = upd_ref[:, 0:2, 2 * N :, :] + from_left[:, :, 2 * N :, :]
    low0a = send_rim(sends_low, corner.at[:, 0], from_above.at[:, 0], low_send.at[1], low_recv.at[1], below)
    low0b = send_rim(sends_low, corner.at[:, 1], from_above.at[:, 1], low_send.at[2], low_recv.at[2], below)

    for copy in y_copies:
        copy.wait_recv()
    slots = 128 * 32
    mine = gathered.at[core, x, pl.ds(z * 4, 4)]
    mine[...] = (y_in[0] + y_in[1] + y_in[2] + y_in[3]) * np.float32(1.0 / math.sqrt(slots))
    zg_copies = [send(mine, mine, zg_send.at[d - 1], zg_recv.at[d - 1], z_peers[d - 1]) for d in (1, 2, 3)]
    top = send_rim(sends_right, upd_ref.at[:, 4:6, :N, :], from_left.at[:, :, :N, :], right_send.at[2], right_recv.at[2], right)

    for copy in zg_copies:
        copy.wait_recv()
    xg_copies = [
        send(gathered.at[core, x], gathered.at[core, x], xg_send.at[d - 1], xg_recv.at[d - 1], x_peers[d - 1])
        for d in (1, 2, 3)
    ]
    cg_copies = [send(gathered.at[core, x], gathered.at[core, x], cg_send.at[0], cg_recv.at[0], partner)]

    def put(b, r0, value):
        for comp in range(2):
            here = (comp, slice(r0, r0 + N), slice(b * H, (b + 1) * H))
            out_ref[here] = obj_ref[here] + value[comp] * scale

    for b in (2, 3):
        put(b, N, upd_ref[:, b, N : 2 * N, :])
    for d in (1, 2, 3):
        xg_copies[d - 1].wait_recv()
        came = (x + 4 - d) % 4
        cg_copies.append(
            send(gathered.at[core, came], gathered.at[core, came], cg_send.at[d], cg_recv.at[d], partner)
        )
    pl.when(has_left)(mid.wait_recv)
    for b in (0, 1):
        put(b, N, upd_ref[:, b, N : 2 * N, :] + from_left[:, b, N : 2 * N, :])
    pl.when(has_above)(low1.wait_recv)
    pl.when(has_above)(low2.wait_recv)
    for b in (2, 3):
        put(b, 0, upd_ref[:, b, :N, :] + from_above[:, b])
    pl.when(has_left)(top.wait_recv)
    for copy in cg_copies:
        copy.wait_recv()
    for h in range(2):
        for xx in range(4):
            for rg in range(8):
                for lg in range(2):
                    grad_ref[h, xx * 64 + rg * 8 : xx * 64 + rg * 8 + 8, lg * H : (lg + 1) * H] = gathered[h, xx, rg * 2 + lg]
    pl.when(has_above)(low0a.wait_recv)
    pl.when(has_above)(low0b.wait_recv)
    for b in (0, 1):
        put(b, 0, upd_ref[:, b, :N, :] + from_left[:, b, :N, :] + from_above[:, b])
    for copy in started:
        copy.wait_send()
    for go, copy in rims:
        pl.when(go)(copy.wait_send)


def exchange(update, object_field, total, probe):
    vmem = pl.BlockSpec(memory_space=pltpu.VMEM)
    f32 = jnp.float32
    dma = pltpu.SemaphoreType.DMA
    return pl.pallas_call(
        exchange_kernel,
        out_shape=(
            jax.ShapeDtypeStruct((2, BLOCK, BLOCK), f32),
            jax.ShapeDtypeStruct((2, N, N), f32),
        ),
        in_specs=[vmem] * 4,
        out_specs=(vmem, vmem),
        scratch_shapes=[
            pltpu.VMEM((2, 2, WIDE, H), f32),
            pltpu.VMEM((2, 4, N, H), f32),
            pltpu.VMEM((2, 2, N, H), f32),
            pltpu.VMEM((N, N), f32),
            pltpu.VMEM((N, N), f32),
            pltpu.VMEM((3, 64, N), f32),
            pltpu.VMEM((16, 8, H), f32),
            pltpu.VMEM((3, 4, 8, H), f32),
            pltpu.VMEM((4, 4, 8, H), f32),
            pltpu.VMEM((2, 4, 16, 8, H), f32),
            dma((3,)), dma((3,)), dma((4,)), dma((4,)), dma((1,)), dma((1,)), dma((3,)), dma((3,)),
            *[dma((3,))] * 8, dma((4,)), dma((4,)),
        ],
        compiler_params=pltpu.CompilerParams(
            collective_id=0, has_side_effects=True, vmem_limit_bytes=32 * 1024 * 1024
        ),
    )(update, object_field, total, probe)


def shards(object_field, probe, amplitudes, corner_rows, corner_cols, counts):
    tables = [jnp.asarray(t) for t in stage_tables()]
    amplitudes = pltpu.with_memory_space_constraint(amplitudes, pltpu.HBM)
    lows, corners = [], []
    for q in range(2):
        rows = slice(q * H, (q + 1) * H)
        lows.append(passed_along(object_field[:, rows, :], "tile", -1))
        corners.append(from_diagonal(object_field[:, rows, :N]))
    right = passed_along(object_field[:, :, :N], "pos", -1)
    fixed = ((corner_rows, corner_cols, counts), amplitudes, tables)
    reach = BLOCK - N
    state = run_slots(
        lambda r, c: (r <= reach) & (c <= reach), ((0, 0),), (object_field,), (probe,), False, *fixed
    )
    state = run_slots(lambda r, c: (r <= reach) & (c > reach), ((0, BLOCK),), (right,), state, False, *fixed)
    for q, rule in enumerate((lambda r, c: (r > reach) & (r <= reach + H), lambda r, c: r > reach + H)):
        row = BLOCK + q * H
        state = run_slots(rule, ((row, 0), (row, BLOCK)), (lows[q], corners[q]), state, q == 1, *fixed)
    _, update, total, _ = state
    return exchange(update, object_field, total.reshape(2 * N, N), probe)


def solution(mesh):
    return jax.shard_map(
        shards,
        mesh=mesh,
        in_specs=(
            P(None, "tile", "pos"),
            P(),
            P("tile", "pos", None, None, None),
            P("tile", "pos", None),
            P("tile", "pos", None),
            P("tile", "pos"),
        ),
        out_specs=(P(None, "tile", "pos"), P()),
        check_vma=False,
    )
```

```python
import functools
import math

import jax
import jax.numpy as jnp
import ml_dtypes
import numpy as np
from jax import lax
from jax.experimental import pallas as pl
from jax.experimental.pallas import tpu as pltpu
from jax.sharding import PartitionSpec as P

N = 256
H = 128
BLOCK = 512
WIDE = 768
LIMIT = 24 * 1024 * 1024


def dft_tables():
    j = np.arange(N)
    angle = (j[:, None] * j[None, :] % N) * (2.0 * np.pi / N)
    re = (np.cos(angle) / np.sqrt(N)).astype(np.float32).astype(ml_dtypes.bfloat16)
    im = (-np.sin(angle) / np.sqrt(N)).astype(np.float32).astype(ml_dtypes.bfloat16)
    return re, im


def stage_tables():
    re, im = dft_tables()

    def pair(a, b, c, d):
        return np.concatenate([np.concatenate([a, b], 1), np.concatenate([c, d], 1)], 0)

    first = [pair(re[:H, q::2], -im[:H, q::2], im[:H, q::2], re[:H, q::2]) for q in (0, 1)]
    second = pair(re, im, -im, re)
    third = [pair(re[q::2, :H], im[q::2, :H], -im[q::2, :H], re[q::2, :H]) for q in (0, 1)]
    fourth = pair(re, -im, im, re)
    return np.stack(first), second, np.stack(third), fourth


def slot_class(r, c):
    reach = BLOCK - N
    lower = 2 + (r > reach + H).astype(jnp.int32)
    return jnp.where(r > reach, lower, (c > reach).astype(jnp.int32))


def slots_kernel(
    stage, places, first, last,
    rows_ref, cols_ref, count_ref, amp_ref, t1_ref, t2_ref, t3_ref, t4_ref, *refs,
):
    n_pieces = len(places)
    pieces = refs[:n_pieces]
    refs = refs[n_pieces:]
    if first:
        probe_ref = refs[0]
    refs = refs[1 if first else 4 :]
    ext, upd_ref, psum_ref, prb = refs[:4]
    pat, ext_b, exit_s, amp_buf = (refs[4 + 4 * i : 8 + 4 * i] for i in range(4))
    near_b, fold_b, back_b, lanes_buf, order, piece_sem, amp_sem = refs[20:]
    copies = []

    def bring(source, target):
        copies.append(pltpu.make_async_copy(source, target, piece_sem.at[len(copies)]))
        copies[-1].start()

    for piece, (r0, c0) in zip(pieces, places):
        _, h, w = piece.shape
        for b in range(w // H):
            bring(piece.at[:, :, b * H : (b + 1) * H], ext.at[:, c0 // H + b, r0 : r0 + h, :])

    def collect(s, carry):
        n, before, best, pick = carry
        live = s < count_ref[0, 0]
        level = slot_class(rows_ref[0, 0, s], cols_ref[0, 0, s])
        earlier = jnp.logical_and(live, level < stage)
        newer = jnp.logical_and(earlier, level >= best)
        order[n + 1] = s
        return (
            n + jnp.logical_and(live, level == stage).astype(jnp.int32),
            before + earlier.astype(jnp.int32),
            jnp.where(newer, level, best),
            jnp.where(newer, s, pick),
        )

    zero = jnp.int32(0)
    total, before, _, pick = lax.fori_loop(0, rows_ref.shape[2], collect, (zero, zero, zero, zero))
    waiting = lax.rem(before, 2)
    order[0] = pick
    base = 1 - waiting
    total = total + waiting
    if not last:
        total = total - lax.rem(total, 2)

    def amp_copy(i, k=0):
        return pltpu.make_async_copy(amp_ref.at[0, 0, order[base + i]], amp_buf[k], amp_sem.at[k])

    final = jnp.maximum(total - 1, 0)
    pairs = (total + 1) // 2

    def fetch(pair, half):
        for m in range(2):
            amp_copy(jnp.minimum(2 * pair + m, final), 2 * half + m).start()

    @pl.when(total > 0)
    def _():
        fetch(0, 0)

    if first:
        for b in range(2):
            bring(probe_ref.at[:, :, b * H : (b + 1) * H], lanes_buf.at[:, b])
        upd_ref[...] = jnp.zeros_like(upd_ref)
        psum_ref[...] = jnp.zeros_like(psum_ref)
    for copy in copies:
        copy.wait()
    if first:
        for comp in range(2):
            for q in range(2):
                for b in range(2):
                    prb[comp, q * H : (q + 1) * H, b * H : (b + 1) * H] = lanes_buf[comp, b, pl.ds(q, H, stride=2), :]

    lane = lax.broadcasted_iota(jnp.int32, (H, H), 1)

    dot = functools.partial(jnp.dot, preferred_element_type=jnp.float32)

    def place(i):
        s = order[base + i]
        c = cols_ref[0, 0, s]
        return rows_ref[0, 0, s], c // H, lax.rem(c, H)

    def enter(i, k, q):
        r, c0, off = place(i)
        back_shift = lax.rem(H - off, H)
        keep = lane < H - off
        part = []
        for comp in range(2):
            blocks = [pltpu.roll(ext[comp, c0 + b, pl.ds(r + q, H, stride=2), :], back_shift, 1) for b in range(3)]
            part.append([jnp.where(keep, blocks[b], blocks[b + 1]) for b in range(2)])
        for b in range(2):
            here = (slice(q * H, (q + 1) * H), slice(b * H, (b + 1) * H))
            pre, pim = prb[(0,) + here], prb[(1,) + here]
            are, aim = part[0][b], part[1][b]
            ere = pre * are - pim * aim
            eim = pre * aim + pim * are
            pat[k][(0,) + here] = are
            pat[k][(1,) + here] = aim
            exit_s[k][(0,) + here] = ere
            exit_s[k][(1,) + here] = eim
            ext_b[k][q, 0:H, b * H : (b + 1) * H] = ere.astype(jnp.bfloat16)
            ext_b[k][q, H:N, b * H : (b + 1) * H] = eim.astype(jnp.bfloat16)

    def near(k, m):
        even = dot(t1_ref[0], ext_b[k][0])
        odd = dot(t1_ref[1], ext_b[k][1])
        for comp in range(2):
            e, o = even[comp * H : (comp + 1) * H], odd[comp * H : (comp + 1) * H]
            near_b[m, 0:H, comp * N : (comp + 1) * N] = (e + o).astype(jnp.bfloat16)
            near_b[m, H:N, comp * N : (comp + 1) * N] = (e - o).astype(jnp.bfloat16)

    def project(k, m):
        far = dot(near_b[m], t2_ref[...])
        fre, fim = far[:, :N], far[:, N:]
        ratio = amp_buf[k][...].astype(jnp.float32) * lax.rsqrt(fre * fre + fim * fim + 0.25)
        for comp, part in enumerate((fre * ratio, fim * ratio)):
            top, low = part[:H], part[H:]
            fold_b[m, 0, comp * H : (comp + 1) * H, :] = (top + low).astype(jnp.bfloat16)
            fold_b[m, 1, comp * H : (comp + 1) * H, :] = (top - low).astype(jnp.bfloat16)

    def back(k, m, q):
        part = dot(t3_ref[q], fold_b[m, q])
        for comp in range(2):
            back_b[m, q * H : (q + 1) * H, comp * N : (comp + 1) * N] = part[comp * H : (comp + 1) * H].astype(
                jnp.bfloat16
            )

    def finish(i, k, m, q, live):
        r, c0, off = place(i)
        here = slice(q * H, (q + 1) * H)
        new = dot(back_b[m, here], t4_ref[...])
        dre = new[:, :N] - exit_s[k][0, here]
        dim = new[:, N:] - exit_s[k][1, here]
        if live is not None:
            dre, dim = dre * live, dim * live
        psum_ref[0, here] += pat[k][0, here] * dre + pat[k][1, here] * dim
        psum_ref[1, here] += pat[k][0, here] * dim - pat[k][1, here] * dre
        pre, pim = prb[0, here], prb[1, here]
        terms = (pre * dre + pim * dim, pre * dim - pim * dre)
        for comp in range(2):
            z0 = pltpu.roll(terms[comp][:, :H], off, 1)
            z1 = pltpu.roll(terms[comp][:, H:], off, 1)
            zero = jnp.zeros_like(z0)
            keep = lane >= off
            for b, val in enumerate((jnp.where(keep, z0, zero), jnp.where(keep, z1, z0), jnp.where(keep, zero, z1))):
                spot = (comp, c0 + b, pl.ds(r + q, H, stride=2), slice(None))
                upd_ref[spot] = upd_ref[spot] + val

    def work(pair, half):
        follow = jnp.minimum(pair + 1, pairs - 1)
        ids = [jnp.minimum(2 * pair + m, final) for m in range(2)]
        nxt = [jnp.minimum(2 * follow + m, final) for m in range(2)]
        live = (2 * pair + 1 < total).astype(jnp.float32)
        for m in range(2):
            amp_copy(ids[m], 2 * half + m).wait()
        for m in range(2):
            near(2 * half + m, m)
        enter(nxt[0], 2 * (1 - half), 0)
        for m in range(2):
            project(2 * half + m, m)
        enter(nxt[0], 2 * (1 - half), 1)
        for m in range(2):
            for q in range(2):
                back(2 * half + m, m, q)
        enter(nxt[1], 2 * (1 - half) + 1, 0)
        for m in range(2):
            for q in range(2):
                finish(ids[m], 2 * half + m, m, q, live if m else None)
        enter(nxt[1], 2 * (1 - half) + 1, 1)

    @pl.when(total > 0)
    def _():
        for m in range(2):
            for q in range(2):
                enter(jnp.minimum(m, final), m, q)

    def step(j, carry):
        for half in range(2):
            pair = 2 * j + half

            def run(pair=pair, half=half):
                @pl.when(pair + 1 < pairs)
                def _():
                    fetch(pair + 1, 1 - half)

                work(pair, half)

            if half == 0:
                run()
            else:
                pl.when(pair < pairs)(run)
        return carry

    lax.fori_loop(0, (pairs + 1) // 2, step, 0)
    if last:
        for comp in range(2):
            for b in range(2):
                lanes = slice(b * H, (b + 1) * H)
                for q in range(2):
                    lanes_buf[comp, b, pl.ds(q, H, stride=2), :] = psum_ref[comp, q * H : (q + 1) * H, lanes]
                psum_ref[comp, :, lanes] = lanes_buf[comp, b]


def run_slots(stage, places, pieces, state, last, scalars, amplitudes, tables):
    smem = pl.BlockSpec(memory_space=pltpu.SMEM)
    vmem = pl.BlockSpec(memory_space=pltpu.VMEM)
    hbm = pl.BlockSpec(memory_space=pl.ANY)
    far = pl.BlockSpec(memory_space=pltpu.HBM)
    first = len(state) == 1
    shapes = [(2, WIDE // H, WIDE, H)] * 2 + [(2, N, N)] * 2
    at = 8 + len(pieces)
    return pl.pallas_call(
        functools.partial(slots_kernel, stage, places, first, last),
        out_shape=tuple(jax.ShapeDtypeStruct(shape, jnp.float32) for shape in shapes),
        in_specs=[smem] * 3 + [far] + [vmem] * 4 + [hbm] * len(pieces) + ([hbm] if first else [vmem] * 4),
        out_specs=(vmem,) * 4,
        input_output_aliases={} if first else {at + i: i for i in range(4)},
        scratch_shapes=[
            *[pltpu.VMEM((2, N, N), jnp.float32)] * 4,
            *[pltpu.VMEM((2, N, N), jnp.bfloat16)] * 4,
            *[pltpu.VMEM((2, N, N), jnp.float32)] * 4,
            *[pltpu.VMEM((N, N), jnp.bfloat16)] * 4,
            pltpu.VMEM((2, N, 2 * N), jnp.bfloat16),
            pltpu.VMEM((2, 2, N, N), jnp.bfloat16),
            pltpu.VMEM((2, N, 2 * N), jnp.bfloat16),
            pltpu.VMEM((2, 2, N, H), jnp.float32),
            pltpu.SMEM((40,), jnp.int32),
            pltpu.SemaphoreType.DMA((2 + sum(p.shape[2] // H for p in pieces),)),
            pltpu.SemaphoreType.DMA((4,)),
        ],
        compiler_params=pltpu.CompilerParams(vmem_limit_bytes=LIMIT),
        cost_estimate=pl.CostEstimate(flops=10_000_000_000, bytes_accessed=4_000_000, transcendentals=0),
    )(*scalars, amplitudes, *tables, *pieces, *state)


def passed_along(block, axis, distance):
    devices = range(lax.axis_size(axis))
    route = [(i - distance, i) for i in devices if i - distance in devices]
    return lax.ppermute(block, axis, route)


def from_diagonal(block):
    wide, tall = lax.axis_size("pos"), lax.axis_size("tile")
    route = [((p + 1) * tall + t + 1, p * tall + t) for p in range(wide - 1) for t in range(tall - 1)]
    return lax.ppermute(block, ("pos", "tile"), route)


def exchange_kernel(
    upd_ref, obj_ref, sum_ref, probe_ref, out_ref, grad_ref,
    from_left, from_above, corner, pair_in, part, x_in, piece, z_in, y_in, gathered,
    right_send, right_recv, low_send, low_recv, pair_send, pair_recv, x_send, x_recv,
    z_send, z_recv, y_send, y_recv, zg_send, zg_recv, xg_send, xg_recv, cg_send, cg_recv,
):
    p = lax.axis_index("pos")
    t = lax.axis_index("tile")
    x, z, core = p // 8, (p // 2) % 4, p % 2

    def pos_of(xx, zz, cc):
        return xx * 8 + zz * 2 + cc

    right = {"pos": (p + 1) % 32, "tile": t}
    left = {"pos": (p + 31) % 32, "tile": t}
    below = {"pos": p, "tile": (t + 1) % 4}
    partner = {"pos": pos_of(x, z, 1 - core), "tile": t}
    x_peers = [{"pos": pos_of((x + d) % 4, z, core), "tile": t} for d in (1, 2, 3)]
    z_peers = [{"pos": pos_of(x, (z + d) % 4, core), "tile": t} for d in (1, 2, 3)]
    y_peers = [{"pos": p, "tile": (t + d) % 4} for d in (1, 2, 3)]

    barrier = pltpu.get_barrier_semaphore()
    peers = [right, left, partner] + x_peers + z_peers + y_peers
    for peer in peers:
        pl.semaphore_signal(barrier, inc=1, device_id=peer, device_id_type=pl.DeviceIdType.MESH)
    pl.semaphore_wait(barrier, len(peers))

    started, rims = [], []
    sends_right, sends_low, has_left, has_above = p < 31, t < 3, p > 0, t > 0

    def describe(source, target, send_sem, recv_sem, peer):
        return pltpu.make_async_remote_copy(
            src_ref=source, dst_ref=target, send_sem=send_sem, recv_sem=recv_sem,
            device_id=peer, device_id_type=pl.DeviceIdType.MESH,
        )

    def send(*where):
        copy = describe(*where)
        copy.start()
        started.append(copy)
        return copy

    def send_rim(go, *where):
        copy = describe(*where)
        pl.when(go)(copy.start)
        rims.append((go, copy))
        return copy

    @pl.when(p == 0)
    def _():
        from_left[...] = jnp.zeros_like(from_left)

    @pl.when(t == 0)
    def _():
        from_above[...] = jnp.zeros_like(from_above)

    edge = send_rim(sends_right, upd_ref.at[:, 4:6, 2 * N :, :], from_left.at[:, :, 2 * N :, :], right_send.at[0], right_recv.at[0], right)
    low1 = send_rim(sends_low, upd_ref.at[:, 2, 2 * N :, :], from_above.at[:, 2], low_send.at[0], low_recv.at[0], below)
    half = send(sum_ref.at[pl.ds((1 - core) * N, N)], pair_in, pair_send.at[0], pair_recv.at[0], partner)
    half.wait_recv()
    part[...] = sum_ref[pl.ds(core * N, N), :] + pair_in[...]
    x_copies = [
        send(part.at[pl.ds(((x + d) % 4) * 64, 64)], x_in.at[d - 1], x_send.at[d - 1], x_recv.at[d - 1], x_peers[d - 1])
        for d in (1, 2, 3)
    ]
    power = jnp.sum(probe_ref[...] * probe_ref[...]) * (1.0 / (N * N)) + 1e-06
    scale = 1.0 / jnp.full((1, H), power, jnp.float32)

    for copy in x_copies:
        copy.wait_recv()
    shard = part[pl.ds(x * 64, 64), :] + x_in[0] + x_in[1] + x_in[2]
    for rg in range(8):
        for lg in range(2):
            piece[rg * 2 + lg] = shard[rg * 8 : rg * 8 + 8, lg * H : (lg + 1) * H]
    z_copies = [
        send(piece.at[pl.ds(((z + d) % 4) * 4, 4)], z_in.at[d - 1], z_send.at[d - 1], z_recv.at[d - 1], z_peers[d - 1])
        for d in (1, 2, 3)
    ]
    low2 = send_rim(sends_low, upd_ref.at[:, 3, 2 * N :, :], from_above.at[:, 3], low_send.at[3], low_recv.at[3], below)
    mid = send_rim(sends_right, upd_ref.at[:, 4:6, N : 2 * N, :], from_left.at[:, :, N : 2 * N, :], right_send.at[1], right_recv.at[1], right)
    for copy in z_copies:
        copy.wait_recv()
    y_in[t] = piece[pl.ds(z * 4, 4)] + z_in[0] + z_in[1] + z_in[2]
    y_copies = [send(y_in.at[t], y_in.at[t], y_send.at[d - 1], y_recv.at[d - 1], y_peers[d - 1]) for d in (1, 2, 3)]
    pl.when(has_left)(edge.wait_recv)
    corner[...] = upd_ref[:, 0:2, 2 * N :, :] + from_left[:, :, 2 * N :, :]
    low0a = send_rim(sends_low, corner.at[:, 0], from_above.at[:, 0], low_send.at[1], low_recv.at[1], below)
    low0b = send_rim(sends_low, corner.at[:, 1], from_above.at[:, 1], low_send.at[2], low_recv.at[2], below)

    for copy in y_copies:
        copy.wait_recv()
    slots = 128 * 32
    mine = gathered.at[core, x, pl.ds(z * 4, 4)]
    mine[...] = (y_in[0] + y_in[1] + y_in[2] + y_in[3]) * np.float32(1.0 / math.sqrt(slots))
    zg_copies = [send(mine, mine, zg_send.at[d - 1], zg_recv.at[d - 1], z_peers[d - 1]) for d in (1, 2, 3)]
    top = send_rim(sends_right, upd_ref.at[:, 4:6, :N, :], from_left.at[:, :, :N, :], right_send.at[2], right_recv.at[2], right)

    for copy in zg_copies:
        copy.wait_recv()
    xg_copies = [
        send(gathered.at[core, x], gathered.at[core, x], xg_send.at[d - 1], xg_recv.at[d - 1], x_peers[d - 1])
        for d in (1, 2, 3)
    ]
    cg_copies = [send(gathered.at[core, x], gathered.at[core, x], cg_send.at[0], cg_recv.at[0], partner)]

    def put(b, r0, value):
        for comp in range(2):
            here = (comp, slice(r0, r0 + N), slice(b * H, (b + 1) * H))
            out_ref[here] = obj_ref[here] + value[comp] * scale

    for b in (2, 3):
        put(b, N, upd_ref[:, b, N : 2 * N, :])
    for d in (1, 2, 3):
        xg_copies[d - 1].wait_recv()
        came = (x + 4 - d) % 4
        cg_copies.append(
            send(gathered.at[core, came], gathered.at[core, came], cg_send.at[d], cg_recv.at[d], partner)
        )
    pl.when(has_left)(mid.wait_recv)
    for b in (0, 1):
        put(b, N, upd_ref[:, b, N : 2 * N, :] + from_left[:, b, N : 2 * N, :])
    pl.when(has_above)(low1.wait_recv)
    pl.when(has_above)(low2.wait_recv)
    for b in (2, 3):
        put(b, 0, upd_ref[:, b, :N, :] + from_above[:, b])
    pl.when(has_left)(top.wait_recv)
    for copy in cg_copies:
        copy.wait_recv()
    for h in range(2):
        for xx in range(4):
            for rg in range(8):
                for lg in range(2):
                    grad_ref[h, xx * 64 + rg * 8 : xx * 64 + rg * 8 + 8, lg * H : (lg + 1) * H] = gathered[h, xx, rg * 2 + lg]
    pl.when(has_above)(low0a.wait_recv)
    pl.when(has_above)(low0b.wait_recv)
    for b in (0, 1):
        put(b, 0, upd_ref[:, b, :N, :] + from_left[:, b, :N, :] + from_above[:, b])
    for copy in started:
        copy.wait_send()
    for go, copy in rims:
        pl.when(go)(copy.wait_send)


def exchange(update, object_field, total, probe):
    vmem = pl.BlockSpec(memory_space=pltpu.VMEM)
    f32 = jnp.float32
    dma = pltpu.SemaphoreType.DMA
    return pl.pallas_call(
        exchange_kernel,
        out_shape=(
            jax.ShapeDtypeStruct((2, BLOCK, BLOCK), f32),
            jax.ShapeDtypeStruct((2, N, N), f32),
        ),
        in_specs=[vmem] * 4,
        out_specs=(vmem, vmem),
        scratch_shapes=[
            pltpu.VMEM((2, 2, WIDE, H), f32),
            pltpu.VMEM((2, 4, N, H), f32),
            pltpu.VMEM((2, 2, N, H), f32),
            pltpu.VMEM((N, N), f32),
            pltpu.VMEM((N, N), f32),
            pltpu.VMEM((3, 64, N), f32),
            pltpu.VMEM((16, 8, H), f32),
            pltpu.VMEM((3, 4, 8, H), f32),
            pltpu.VMEM((4, 4, 8, H), f32),
            pltpu.VMEM((2, 4, 16, 8, H), f32),
            dma((3,)), dma((3,)), dma((4,)), dma((4,)), dma((1,)), dma((1,)), dma((3,)), dma((3,)),
            *[dma((3,))] * 8, dma((4,)), dma((4,)),
        ],
        compiler_params=pltpu.CompilerParams(
            collective_id=0, has_side_effects=True, vmem_limit_bytes=32 * 1024 * 1024
        ),
    )(update, object_field, total, probe)


def shards(object_field, probe, amplitudes, corner_rows, corner_cols, counts):
    tables = [jnp.asarray(t) for t in stage_tables()]
    amplitudes = pltpu.with_memory_space_constraint(amplitudes, pltpu.HBM)
    lows, corners = [], []
    for q in range(2):
        rows = slice(q * H, (q + 1) * H)
        lows.append(passed_along(object_field[:, rows, :], "tile", -1))
        corners.append(from_diagonal(object_field[:, rows, :N]))
    right = passed_along(object_field[:, :, :N], "pos", -1)
    fixed = ((corner_rows, corner_cols, counts), amplitudes, tables)
    state = run_slots(0, ((0, 0),), (object_field,), (probe,), False, *fixed)
    state = run_slots(1, ((0, BLOCK),), (right,), state, False, *fixed)
    for q in range(2):
        row = BLOCK + q * H
        state = run_slots(2 + q, ((row, 0), (row, BLOCK)), (lows[q], corners[q]), state, q == 1, *fixed)
    _, update, total, _ = state
    return exchange(update, object_field, total.reshape(2 * N, N), probe)


def solution(mesh):
    return jax.shard_map(
        shards,
        mesh=mesh,
        in_specs=(
            P(None, "tile", "pos"),
            P(),
            P("tile", "pos", None, None, None),
            P("tile", "pos", None),
            P("tile", "pos", None),
            P("tile", "pos"),
        ),
        out_specs=(P(None, "tile", "pos"), P()),
        check_vma=False,
    )
```
